512 devices in a mesh: dom: 64 (over x, z), cell: 8 (over y, core).
Axes of the slice: x: 4, y: 4, z: 16, core: 2. Of those that a mesh axis runs over, the one named last changes fastest.
Arguments:
- features: bfloat16 [131072, 128], P(('cell', 'dom')), parts along dimension 0, may hold values from -6 to 6
- positions: float32 [3, 131072], P(None, ('cell', 'dom')), parts along dimension 1, may hold values from 0 to 320, as said below
- neighbours: int32 [131072, 64], P(('cell', 'dom')), parts along dimension 0, may hold values from 0 to 767, as said below
- neighbour_count: int32 [131072], P(('cell', 'dom')), parts along dimension 0, may hold values from 16 to 64, as said below
- ghost_sends: int32 [2, 131072], P(None, ('cell', 'dom')), parts along dimension 1, may hold values from 0 to 255, as said below
- species: int32 [131072], P(('cell', 'dom')), parts along dimension 0, may hold values from 0 to 5
- wave_index: int32 [3, 1024], replicated, may hold values from -8 to 8, as said below
- force_ref: float32 [3, 131072], P(None, ('cell', 'dom')), parts along dimension 1, may hold values from -6 to 6
- radial_weight: bfloat16 [16, 128], replicated, may hold values from -1.5 to 1.5
- mix_weight: bfloat16 [128, 128], replicated, may hold values from -0.5 to 0.5
- charge_weight: bfloat16 [128, 64], replicated, may hold values from -0.5 to 0.5
- species_charge: float32 [6, 64], replicated, may hold values from -4 to 4
Outputs:
- forces: float32 [3, 131072], P(None, ('cell', 'dom')), parts along dimension 1
- radial_step: float32 [128, 128], P('cell'), parts along dimension 0
- mix_step: float32 [1024, 128], P('cell'), parts along dimension 0
- charge_step: float32 [1024, 64], P('cell'), parts along dimension 0
- species_step: float32 [48, 64], P('cell'), parts along dimension 0
The draws below stay inside these ranges and needn't reach their ends.
There are 8 independent parts, one for each index of `cell`. The reference program is written for one: setup_inputs(seed, part) draws one part's arguments, and reference() takes and returns one part's arrays. A program takes and returns all parts, laid end to end along the dimension named above; an argument that names none is the same for every part. Nothing has to cross between parts.
Inputs may be any that keep to these rules, and one draw needn't show every extreme that they name: `neighbours`: in the shard of domain d, an entry e below 256 names the domain's own atom e; 256 + g names the atom at position g of row 1 of ghost_sends of domain d - 1; 512 + g names the atom at position g of row 0 of ghost_sends of domain d + 1 (domains cyclic). Entries of a row are distinct and never the atom itself. `neighbour_count`: slots below the count are live; in every domain some atom has all 64 slots live. `ghost_sends`: positions within the domain's shard; the entries of one row of one domain are distinct. `wave_index`: columns are distinct and their first component is 1 or more. `positions`: coordinates in a periodic box of 320 along the first axis and 20 along the other two.
All inputs are finite; a program needn't handle non-finite values.
Results may differ from the reference program's by a relative error of at most 0.0051.
Values may be sent and summed in bfloat16 or wider, within the bound.
A program may use at most 64 MiB of HBM per device.

```python
import jax
import jax.numpy as jnp
import numpy as np
from jax import lax

C = 128
Q = 64
K = 1024
NRBF = 16
NB = 64
SPEC = 6
GHOST = 256
ATOM_DEV = 256
ATOMS = 16384


def offset_table():
    rows_list = []
    for step_x in range(-4, 5):
        for step_y in range(-2, 3):
            for step_z in range(-2, 3):
                if step_x != 0 or step_y != 0 or step_z != 0:
                    if step_x * step_x + 4 * (step_y * step_y + step_z * step_z) <= 20:
                        rows_list.append((step_x, step_y, step_z))
    return np.array(rows_list, dtype=np.int32)


def lattice_layout(key):
    domains = ATOMS // ATOM_DEV
    layers = ATOM_DEV // 64
    ghost_layers = GHOST // 64
    order_scores = jax.random.randint(jax.random.fold_in(key, 101), (domains, ATOM_DEV), 0, 1 << 16) * ATOM_DEV + jnp.arange(ATOM_DEV, dtype=jnp.int32)
    site_of_slot = jnp.argsort(order_scores, axis=1).astype(jnp.int32)
    slot_of_site = jnp.argsort(site_of_slot, axis=1).astype(jnp.int32)
    ghost_scores = jax.random.randint(jax.random.fold_in(key, 102), (domains, 2, GHOST), 0, 1 << 16) * GHOST + jnp.arange(GHOST, dtype=jnp.int32)
    ghost_order = jnp.argsort(ghost_scores, axis=2).astype(jnp.int32)
    ghost_rank = jnp.argsort(ghost_order, axis=2).astype(jnp.int32)
    sends_low = jnp.take_along_axis(slot_of_site, ghost_order[:, 0, :], axis=1)
    sends_high = jnp.take_along_axis(slot_of_site, ATOM_DEV - GHOST + ghost_order[:, 1, :], axis=1)
    sends = jnp.stack([sends_low, sends_high], axis=0).reshape(2, domains * GHOST)
    offsets = jnp.asarray(offset_table())
    options_count = offsets.shape[0]
    pick_scores = jax.random.randint(jax.random.fold_in(key, 103), (domains, ATOM_DEV, options_count), 0, 1 << 16) * options_count + jnp.arange(options_count, dtype=jnp.int32)
    picked = jnp.argsort(pick_scores, axis=2)[:, :, :NB]
    moves = offsets[picked]
    sites = site_of_slot[:, :, None]
    target = sites // 64 + moves[..., 0]
    new_y = (sites // 8 % 8 + moves[..., 1]) % 8
    new_z = (sites % 8 + moves[..., 2]) % 8
    column = new_y * 8 + new_z
    inside_site = jnp.clip(target, 0, layers - 1) * 64 + column
    inside = jnp.take_along_axis(slot_of_site, inside_site.reshape(domains, -1), axis=1).reshape(target.shape)
    domain_ids = jnp.arange(domains, dtype=jnp.int32)[:, None, None]
    lower_domain = (domain_ids - 1) % domains
    upper_domain = (domain_ids + 1) % domains
    low_offset = jnp.clip(target + ghost_layers, 0, ghost_layers - 1) * 64 + column
    high_offset = jnp.clip(target - layers, 0, ghost_layers - 1) * 64 + column
    from_lower = ATOM_DEV + ghost_rank[:, 1, :][lower_domain, low_offset]
    from_upper = ATOM_DEV + GHOST + ghost_rank[:, 0, :][upper_domain, high_offset]
    listed = jnp.where(target < 0, from_lower, jnp.where(target >= layers, from_upper, inside))
    lowest = jax.random.randint(jax.random.fold_in(key, 104), (domains, 1), NB // 4, NB + 1)
    spread = jax.random.randint(jax.random.fold_in(key, 105), (domains, ATOM_DEV), 0, NB + 1)
    counts = lowest + spread % (NB - lowest + 1)
    counts = counts.at[:, 0].set(NB)
    return (site_of_slot, sends.astype(jnp.int32), listed.reshape(ATOMS, NB).astype(jnp.int32), counts.reshape(ATOMS).astype(jnp.int32))


def draw_neighbours(key, part):
    return lattice_layout(key)[2]


def draw_neighbour_count(key, part):
    return lattice_layout(key)[3]


def draw_ghost_sends(key, part):
    return lattice_layout(key)[1]


def draw_positions(key, part):
    domains = ATOMS // ATOM_DEV
    layers = ATOM_DEV // 64
    sites = lattice_layout(key)[0]
    domain_ids = jnp.arange(domains, dtype=jnp.int32)[:, None]
    base_x = ((domain_ids * layers + sites // 64).astype(jnp.float32) + 0.5) * 1.25
    base_y = ((sites // 8 % 8).astype(jnp.float32) + 0.5) * 2.5
    base_z = ((sites % 8).astype(jnp.float32) + 0.5) * 2.5
    jitter_key = jax.random.fold_in(key, 201)
    jitter = jax.random.uniform(jitter_key, (3, domains, ATOM_DEV), jnp.float32, -0.3, 0.3)
    coords = jnp.stack([base_x, base_y, base_z], axis=0) + jitter
    return coords.reshape(3, ATOMS).astype(jnp.float32)


def draw_wave_index(key, part):
    scores = jax.random.randint(jax.random.fold_in(key, 301), (2048,), 0, 1 << 16) * 2048 + jnp.arange(2048, dtype=jnp.int32)
    chosen = jnp.argsort(scores)[:K].astype(jnp.int32)
    along_x = 1 + chosen // 256
    along_y = chosen // 16 % 16 - 8
    along_z = chosen % 16 - 8
    return jnp.stack([along_x, along_y, along_z], axis=0).astype(jnp.int32)


def with_ends(entries, stream_key, least, largest):
    index_at = [jax.random.randint(jax.random.fold_in(stream_key, axis), (), 0, length) for axis, length in enumerate(entries.shape)]
    longest = entries.shape.index(max(entries.shape))
    beside = index_at[:longest] + [(index_at[longest] + 1) % entries.shape[longest]] + index_at[longest + 1:]
    return entries.at[tuple(index_at)].set(least).at[tuple(beside)].set(largest)


def steps_of(stream_key, dims, shards, low, high):
    factor_of, own = 1.0, jax.random.fold_in(stream_key, 6)
    for dim, shards_of in shards:
        steps = jnp.exp(jax.random.uniform(jax.random.fold_in(own, dim), (shards_of,), jnp.float32, low / len(shards), high / len(shards)))
        factor_of = factor_of * jnp.repeat(steps, dims[dim] // shards_of).reshape([-1 if axis == dim else 1 for axis in range(len(dims))])
    return factor_of


def gaussian(key, dims, scale, reach, shards=(), kind=jnp.bfloat16):
    values = scale * jax.random.normal(key, dims, jnp.float32)
    if shards:
        values = values * steps_of(key, dims, shards, -0.22, 0.18)
    return jnp.clip(values, -reach, reach).astype(kind)


def setup_inputs(seed: int = 0, part: int = 0) -> dict:
    key_of = jax.random.split(jax.random.key(seed), 13)
    part_splits = jax.random.split(jax.random.fold_in(key_of[12], part), 13)
    features = gaussian(part_splits[0], (ATOMS, C), 1.0, 6.0, ((0, 64),))
    positions = draw_positions(jax.random.fold_in(jax.random.fold_in(key_of[12], part), 71), part)
    neighbours = draw_neighbours(jax.random.fold_in(jax.random.fold_in(key_of[12], part), 71), part)
    neighbour_count = draw_neighbour_count(jax.random.fold_in(jax.random.fold_in(key_of[12], part), 71), part)
    ghost_sends = draw_ghost_sends(jax.random.fold_in(jax.random.fold_in(key_of[12], part), 71), part)
    species = with_ends(jax.random.randint(part_splits[5], (ATOMS,), 0, SPEC), jax.random.fold_in(part_splits[5], 1), 0, SPEC - 1).astype(jnp.int32)
    wave_index = draw_wave_index(jax.random.fold_in(key_of[12], 71), part)
    force_ref = gaussian(part_splits[7], (3, ATOMS), 1.0, 6.0, ((1, 64),), jnp.float32)
    radial_weight = gaussian(key_of[8], (NRBF, C), NRBF ** -0.5, 1.5)
    mix_weight = gaussian(key_of[9], (C, C), C ** -0.5, 0.5)
    charge_weight = gaussian(key_of[10], (C, Q), C ** -0.5, 0.5)
    species_charge = gaussian(key_of[11], (SPEC, Q), 1.0, 4.0, (), jnp.float32)
    return {"features": features, "positions": positions, "neighbours": neighbours, "neighbour_count": neighbour_count, "ghost_sends": ghost_sends, "species": species, "wave_index": wave_index, "force_ref": force_ref, "radial_weight": radial_weight, "mix_weight": mix_weight, "charge_weight": charge_weight, "species_charge": species_charge}


cutoff_radius = 5.0
kernel_width = 1.0
basis_width = 0.5
box_side = 20.0
two_pi = 6.283185307179586
highest = lax.Precision.HIGHEST

def contract_first(left, right):
    return lax.dot_general(left, right, (((0,), (0,)), ((), ())), precision=highest, preferred_element_type=jnp.float32)

def contract_last(left, right):
    return lax.dot_general(left, right, (((1,), (1,)), ((), ())), precision=highest, preferred_element_type=jnp.float32)

def product(left, right):
    return jnp.dot(left, right, precision=highest, preferred_element_type=jnp.float32)

def edge_terms(own_coords, other_coords, live_count, box_lengths, basis_count):
    slots_count = other_coords.shape[2]
    displacement = other_coords - own_coords[:, :, None]
    displacement = displacement - box_lengths[:, None, None] * jnp.floor(displacement / box_lengths[:, None, None] + 0.5)
    distance = jnp.sqrt(lax.optimization_barrier(jnp.sum(displacement * displacement, axis=0)))
    is_live = (jnp.arange(slots_count, dtype=jnp.int32)[None, :] < live_count[:, None]).astype(jnp.float32)
    cutoff_fade = 0.5 * (jnp.cos(jnp.pi * jnp.minimum(distance, cutoff_radius) / cutoff_radius) + 1.0)
    centers = 0.5 + (cutoff_radius - 0.5) * jnp.arange(basis_count, dtype=jnp.float32) / (basis_count - 1)
    basis_rows = jnp.exp(-jnp.square((distance[..., None] - centers) / basis_width)).astype(jnp.bfloat16)
    return (basis_rows, is_live * cutoff_fade)

def silu_slope(value):
    sigmoid = jax.nn.sigmoid(value)
    return sigmoid * (1.0 + value * (1.0 - sigmoid))

def normalized(gradient):
    return gradient / jnp.sqrt(jnp.mean(gradient * gradient) + 1e-06)

def global_slots(neighbours, ghost_sends):
    domains = ATOMS // ATOM_DEV
    owner = (jnp.arange(ATOMS, dtype=jnp.int32) // ATOM_DEV)[:, None]
    lower = (owner - 1) % domains
    upper = (owner + 1) % domains
    low_slot = jnp.clip(neighbours - ATOM_DEV, 0, GHOST - 1)
    high_slot = jnp.clip(neighbours - ATOM_DEV - GHOST, 0, GHOST - 1)
    from_lower = lower * ATOM_DEV + ghost_sends[1][lower * GHOST + low_slot]
    from_upper = upper * ATOM_DEV + ghost_sends[0][upper * GHOST + high_slot]
    local = owner * ATOM_DEV + jnp.clip(neighbours, 0, ATOM_DEV - 1)
    return jnp.where(neighbours < ATOM_DEV, local, jnp.where(neighbours < ATOM_DEV + GHOST, from_lower, from_upper)).astype(jnp.int32)

def reference(features, positions, neighbours, neighbour_count, ghost_sends, species, wave_index, force_ref, radial_weight, mix_weight, charge_weight, species_charge):
    width = features.shape[1]
    slots_count = neighbours.shape[1]
    basis_count = radial_weight.shape[0]
    charges_width = charge_weight.shape[1]
    blocks = ATOMS // ATOM_DEV
    box_lengths = jnp.array([1.25 * ATOMS / 64, box_side, box_side], dtype=jnp.float32)
    slot_blocks = global_slots(neighbours, ghost_sends).reshape(blocks, ATOM_DEV, slots_count)
    own_blocks = positions.reshape(3, blocks, ATOM_DEV).transpose(1, 0, 2)
    count_blocks = neighbour_count.reshape(blocks, ATOM_DEV)

    def message_block(block_args):
        slot_rows, own_coords, live_count = block_args
        basis_rows, edge_weight = edge_terms(own_coords, positions[:, slot_rows], live_count, box_lengths, basis_count)
        filters = jnp.dot(basis_rows.reshape(-1, basis_count), radial_weight, preferred_element_type=jnp.float32)
        filters = filters.reshape(ATOM_DEV, slots_count, width)
        return lax.optimization_barrier(jnp.sum(edge_weight[..., None] * filters * features[slot_rows].astype(jnp.float32), axis=1))
    messages = lax.map(message_block, (slot_blocks, own_blocks, count_blocks)).reshape(ATOMS, width).astype(jnp.bfloat16)
    before = jnp.dot(messages, mix_weight, preferred_element_type=jnp.float32)
    hidden = (features.astype(jnp.float32) + jax.nn.silu(before)).astype(jnp.bfloat16)
    charges = jnp.dot(hidden, charge_weight, preferred_element_type=jnp.float32) + species_charge[species]
    wave_vectors = two_pi * wave_index.astype(jnp.float32) / box_lengths[:, None]
    damping = jnp.exp(-0.5 * kernel_width * kernel_width * lax.optimization_barrier(jnp.sum(wave_vectors * wave_vectors, axis=0))) / ATOMS
    charge_blocks = charges.reshape(blocks, ATOM_DEV, charges_width)

    def structure_block(block_args):
        own_coords, block_charges = block_args
        phases = contract_first(own_coords, wave_vectors)
        return jnp.concatenate([contract_first(jnp.cos(phases), block_charges), contract_first(jnp.sin(phases), block_charges)], axis=1)
    structure = lax.optimization_barrier(jnp.sum(lax.map(structure_block, (own_blocks, charge_blocks)), axis=0))
    coefficients = damping[:, None] * structure

    def force_block(block_args):
        own_coords, block_charges = block_args
        phases = contract_first(own_coords, wave_vectors)
        along_cos = contract_last(block_charges, coefficients[:, :charges_width])
        along_sin = contract_last(block_charges, coefficients[:, charges_width:])
        mixture = jnp.sin(phases) * along_cos - jnp.cos(phases) * along_sin
        return contract_last(wave_vectors, mixture)
    forces = lax.map(force_block, (own_blocks, charge_blocks)).transpose(1, 0, 2).reshape(3, ATOMS)
    errors = 2.0 * (forces - force_ref)
    error_blocks = errors.reshape(3, blocks, ATOM_DEV).transpose(1, 0, 2)

    def gradient_block(block_args):
        own_coords, block_charges, block_errors = block_args
        phases = contract_first(own_coords, wave_vectors)
        cosines = jnp.cos(phases)
        sines = jnp.sin(phases)
        slopes = contract_first(block_errors, wave_vectors)
        direct = product(slopes * sines, coefficients[:, :charges_width]) - product(slopes * cosines, coefficients[:, charges_width:])
        wave_term = jnp.concatenate([contract_first(slopes * sines, block_charges), -contract_first(slopes * cosines, block_charges)], axis=1)
        return (direct, wave_term)
    direct, wave_terms = lax.map(gradient_block, (own_blocks, charge_blocks, error_blocks))
    gradient_waves = lax.optimization_barrier(jnp.sum(wave_terms, axis=0))
    back_waves = damping[:, None] * gradient_waves

    def indirect_block(own_coords):
        phases = contract_first(own_coords, wave_vectors)
        return product(jnp.cos(phases), back_waves[:, :charges_width]) + product(jnp.sin(phases), back_waves[:, charges_width:])
    indirect = lax.map(indirect_block, own_blocks)
    charge_grad = direct.reshape(ATOMS, charges_width) + indirect.reshape(ATOMS, charges_width)
    charge_rounded = charge_grad.astype(jnp.bfloat16)
    charge_sum = contract_first(hidden, charge_rounded)
    one_hot = (species[:, None] == jnp.arange(SPEC, dtype=jnp.int32)[None, :]).astype(jnp.float32)
    species_sum = contract_first(one_hot, charge_grad)
    upstream = contract_last(charge_rounded, charge_weight)
    before_grad = (upstream * silu_slope(before)).astype(jnp.bfloat16)
    mix_sum = contract_first(messages, before_grad)
    message_grad = contract_last(before_grad, mix_weight).astype(jnp.bfloat16)

    def radial_block(running, block_args):
        slot_rows, own_coords, live_count, rows_grad = block_args
        basis_rows, edge_weight = edge_terms(own_coords, positions[:, slot_rows], live_count, box_lengths, basis_count)
        edge_term = (edge_weight[..., None] * rows_grad.astype(jnp.float32)[:, None, :] * features[slot_rows].astype(jnp.float32)).astype(jnp.bfloat16)
        return (running + contract_first(basis_rows.reshape(-1, basis_count), edge_term.reshape(-1, width)), None)
    radial_sum, _ = lax.scan(radial_block, jnp.zeros((basis_count, width), jnp.float32), (slot_blocks, own_blocks, count_blocks, message_grad.reshape(blocks, ATOM_DEV, width)))
    return (forces, normalized(radial_sum), normalized(mix_sum), normalized(charge_sum), normalized(species_sum))
```

```python
import math

import jax
import jax.numpy as jnp
from jax import lax
from jax.experimental import pallas as pl
from jax.experimental.pallas import tpu as pltpu
from jax.sharding import PartitionSpec as P

f32 = jnp.float32
bf16 = jnp.bfloat16
MESH = pl.DeviceIdType.MESH

ATOM = 256
CHAN = 128
CHARGES = 64
WAVES = 1024
SLOTS = 64
BASIS = 16
SPECIES = 6
TABLE = 3 * ATOM
NX = 4
NZ = 16
DOMS = NX * NZ
TOTAL = ATOM * DOMS
XROWS = WAVES // NX
ZROWS = XROWS // NZ
PACK = 256
PROWS = PACK // NZ
SIDES = (1.25 * TOTAL / 64, 20.0, 20.0)
CUTOFF = 5.0
SPREAD = 2.0 * math.sqrt(math.log2(math.e))
CENTERS = [0.5 + 4.5 * b / 15 for b in range(BASIS)]
COS_QUARTER = [(-1.0) ** n * (math.pi / 2) ** (2 * n) / math.factorial(2 * n) for n in range(8)]
SIN_HALF = [(-1.0) ** n * math.pi ** (2 * n + 1) / math.factorial(2 * n + 1) for n in range(8)]
COS_HALF = [(-1.0) ** n * math.pi ** (2 * n) / math.factorial(2 * n) for n in range(9)]


def nn(left, right):
    return lax.dot_general(left, right, (((1,), (0,)), ((), ())), preferred_element_type=f32)


def nt(left, right):
    return lax.dot_general(left, right, (((1,), (1,)), ((), ())), preferred_element_type=f32)


def split(value):
    high = value.astype(bf16)
    return high, (value - high.astype(f32)).astype(bf16)


def poly(coeffs, square):
    total = jnp.full_like(square, coeffs[-1])
    for coeff in reversed(coeffs[:-1]):
        total = total * square + coeff
    return total


def iota(shape, dim):
    return lax.broadcasted_iota(jnp.int32, shape, dim)


def sum_all(value):
    return jnp.sum(jnp.sum(value, axis=1, keepdims=True), axis=0, keepdims=True)


def kernel(
    feat_ref, pos_ref, nbr_ref, cnt_ref, ghost_ref, spec_ref, wave_ref, fref_ref,
    rw_ref, mw_ref, cw_ref, sc_ref,
    forces_ref, rstep_ref, mstep_ref, cstep_ref, sstep_ref,
    wpad, wcol, ppad, pcol, tpad, cos_ref, sin_ref, idx_ref, bit_ref, word_ref,
    m_ref, ml_ref, g_ref, outf, outp, gf, gp,
    w1h, w1l, w2h, w2l, t1h, t1l, t2h, t2l, mix_ref, dir_ref,
    sx, rx, xown, sz, rz, res, sg, pk, rz3, xb3, res3,
    gsend, grecv, xsend, xrecv, zsend, zrecv, asend, arecv, bsend, brecv,
    z3send, z3recv, x3send, x3recv, a3send, a3recv,
):
    me = lax.axis_index("dom")
    xi = lax.div(me, NZ)
    zi = lax.rem(me, NZ)
    upper = lax.rem(me + 1, DOMS)
    lower = lax.rem(me + DOMS - 1, DOMS)

    def xpeer(off):
        return lax.rem(xi + off, NX) * NZ + zi

    def zat(off):
        return lax.rem(zi + off, NZ)

    def zpeer(off):
        return xi * NZ + zat(off)

    barrier = pltpu.get_barrier_semaphore()

    def greet(target):
        pl.semaphore_signal(barrier, inc=1, device_id={"dom": target}, device_id_type=MESH)

    def greet_z(off, carry):
        greet(zpeer(off))
        return carry

    lax.fori_loop(1, NZ, greet_z, 0)
    for off in range(1, NX):
        greet(xpeer(off))
    greet(upper)
    greet(lower)

    def remote(src, dst, send, recv, target):
        return pltpu.make_async_remote_copy(
            src_ref=src, dst_ref=dst, send_sem=send, recv_sem=recv,
            device_id={"dom": target}, device_id_type=MESH,
        )

    ft32 = feat_ref[...].astype(f32).T
    ftb = ft32.astype(bf16)
    tpad[...] = jnp.zeros_like(tpad)
    ppad[...] = jnp.zeros_like(ppad)
    ppad[0:3, :] = pos_ref[...]
    own8 = ppad[0:8, :]
    pcol[0:ATOM, :] = ppad[...].T
    p1 = own8.astype(bf16)
    p2 = (own8 - p1.astype(f32)).astype(bf16)
    p3 = (own8 - p1.astype(f32) - p2.astype(f32)).astype(bf16)
    rows_of = iota((ATOM, ATOM), 0)
    for r in range(2):
        perm = jnp.where(rows_of == ghost_ref[r : r + 1, :], 1.0, 0.0).astype(bf16)
        outf[r] = nn(ftb, perm).astype(bf16)
        outp[r] = nn(p1, perm) + nn(p2, perm) + nn(p3, perm)

    pl.semaphore_wait(barrier, NZ - 1 + NX - 1 + 2)

    ghost_copies = []
    for r, target in ((1, upper), (0, lower)):
        slot = 1 - r
        ghost_copies.append(
            remote(outp.at[r], gp.at[slot], gsend.at[2 * slot], grecv.at[2 * slot], target)
        )
        ghost_copies.append(
            remote(outf.at[r], gf.at[slot], gsend.at[2 * slot + 1], grecv.at[2 * slot + 1], target)
        )
    for copy in ghost_copies:
        copy.start()

    wave = wave_ref[...].astype(f32)
    wpad[...] = jnp.zeros_like(wpad)
    wpad[0:3, :] = wave
    steps = [2.0 * math.pi / side for side in SIDES]
    square = sum((wave[a : a + 1, :] * steps[a]) ** 2 for a in range(3))
    wpad[3:4, :] = jnp.exp(-0.5 * square) * (1.0 / TOTAL)
    wcol[...] = wpad[...].T

    pos = pos_ref[...]
    px, py, pz = (pos[a : a + 1, :] for a in range(3))
    tx, ty, tz = (pos[a : a + 1, :] * (1.0 / SIDES[a]) for a in range(3))

    def phase_block(step, carry):
        rows = pl.ds(pl.multiple_of(step * 32, 32), 32)
        cols = wcol[rows, :]
        turns = cols[:, 0:1] * tx + cols[:, 1:2] * ty + cols[:, 2:3] * tz
        turns = turns - jnp.floor(turns + 0.5)
        sq = turns * turns
        half_sin = turns * poly(SIN_HALF, sq)
        half_cos = poly(COS_HALF, sq)
        cos_ref[rows, :] = 1.0 - 2.0 * half_sin * half_sin
        sin_ref[rows, :] = 2.0 * half_sin * half_cos
        return carry

    lax.fori_loop(0, WAVES // 32, phase_block, 0)

    tpad[:, 0:SLOTS] = nbr_ref[0:128, :].astype(f32)
    left = tpad[...].T[0:SLOTS, :]
    tpad[:, 0:SLOTS] = nbr_ref[128:256, :].astype(f32)
    right = tpad[...].T[0:SLOTS, :]
    entries = jnp.concatenate([left, right], axis=1).astype(jnp.int32)
    live = iota((SLOTS, ATOM), 0) < cnt_ref[...]
    idx_ref[...] = jnp.where(live, lax.shift_right_logical(entries, 5), -1)
    bit_ref[...] = lax.shift_left(jnp.ones_like(entries), entries & 31)
    word_rows = iota((TABLE // 32, ATOM), 0)

    def word_step(n, words):
        hit = word_rows == idx_ref[pl.ds(n, 1), :]
        return words | jnp.where(hit, bit_ref[pl.ds(n, 1), :], 0)

    word_ref[...] = lax.fori_loop(
        0, SLOTS, word_step, jnp.zeros((TABLE // 32, ATOM), jnp.int32)
    )
    shifts = iota((32, ATOM), 0)

    def edge_block(step, carry):
        rows = pl.ds(pl.multiple_of(step * 32, 32), 32)
        cols = pcol[rows, :]
        dist2 = jnp.zeros((32, ATOM), f32)
        for a, own in enumerate((px, py, pz)):
            delta = cols[:, a : a + 1] - own
            delta = delta - SIDES[a] * jnp.floor(delta * (1.0 / SIDES[a]) + 0.5)
            dist2 = dist2 + delta * delta
        dist = jnp.sqrt(dist2)
        part = jnp.minimum(dist, CUTOFF) * (1.0 / CUTOFF)
        fade = poly(COS_QUARTER, part * part)
        mask = lax.shift_right_logical(
            jnp.broadcast_to(word_ref[pl.ds(step, 1), :], (32, ATOM)), shifts
        ) & 1
        weight = fade * fade * mask.astype(f32)
        scaled = dist * SPREAD
        for b in range(BASIS):
            away = scaled - SPREAD * CENTERS[b]
            basis = jnp.exp2(-(away * away)).astype(bf16)
            m_ref[b, rows, :], ml_ref[b, rows, :] = split(basis.astype(f32) * weight)
        return carry

    lax.fori_loop(0, ATOM // 32, edge_block, 0)

    for copy in ghost_copies:
        copy.wait_recv()
    for slot in range(2):
        ppad[0:8, :] = gp[slot]
        pcol[(1 + slot) * ATOM : (2 + slot) * ATOM, :] = ppad[...].T
    lax.fori_loop(ATOM // 32, TABLE // 32, edge_block, 0)

    tpad[...] = jnp.zeros_like(tpad)
    tpad[0:BASIS, :] = rw_ref[...].astype(f32)
    radial = tpad[...].T
    messages = jnp.zeros((CHAN, ATOM), f32)
    for b in range(BASIS):
        gathered = jnp.zeros((CHAN, ATOM), f32)
        for part in (m_ref, ml_ref):
            gathered = (
                gathered
                + nn(ftb, part[b, 0:ATOM, :])
                + nn(gf[0], part[b, ATOM : 2 * ATOM, :])
                + nn(gf[1], part[b, 2 * ATOM : TABLE, :])
            )
        g_ref[b] = gathered
        messages = messages + radial[:, b : b + 1] * gathered
    messages_b = messages.astype(bf16)
    mixT = mw_ref[...].astype(f32).T.astype(bf16)
    before = nn(mixT, messages_b)
    sigmoid = 1.0 / (1.0 + jnp.exp(-before))
    hidden_b = (ft32 + before * sigmoid).astype(bf16)
    slope = sigmoid * (1.0 + before * (1.0 - sigmoid))
    tpad[:, 0:CHARGES] = cw_ref[...].astype(f32)
    cwT = tpad[...].T[0:CHARGES, :].astype(bf16)
    tpad[...] = jnp.zeros_like(tpad)
    tpad[0:SPECIES, 0:CHARGES] = sc_ref[...]
    offsets = tpad[...].T[0:CHARGES, :]
    species = spec_ref[...]
    charges = nn(cwT, hidden_b)
    added = jnp.zeros((CHARGES, ATOM), f32)
    for s in range(SPECIES):
        added = jnp.where(species == s, offsets[:, s : s + 1], added)
    charges = charges + added
    qh, ql = split(charges)
    zero = jnp.zeros((CHARGES, ATOM), bf16)
    w1h[0:CHARGES, :] = qh
    w1h[CHARGES:CHAN, :] = zero
    w1l[0:CHARGES, :] = ql
    w1l[CHARGES:CHAN, :] = zero
    w2h[0:CHARGES, :] = zero
    w2h[CHARGES:CHAN, :] = qh
    w2l[0:CHARGES, :] = zero
    w2l[CHARGES:CHAN, :] = ql
    for source, target in ((w1h, t1h), (w1l, t1l), (w2h, t2h), (w2l, t2l)):
        target[...] = source[...].astype(f32).T.astype(bf16)

    def both(first, second, negate):
        fh, fl = split(first)
        sh, sl = split(second)
        one = nn(fh, t1h[...]) + nn(fh, t1l[...]) + nn(fl, t1h[...])
        two = nn(sh, t2h[...]) + nn(sh, t2l[...]) + nn(sl, t2h[...])
        return one - two if negate else one + two

    def chunk_rows(off):
        return pl.ds(pl.multiple_of(lax.rem(xi + off, NX) * XROWS, XROWS), XROWS)

    def z_rows(off):
        return pl.ds(pl.multiple_of(zat(off) * ZROWS, ZROWS), ZROWS)

    def res_rows(off):
        return pl.ds(pl.multiple_of(xi * XROWS + zat(off) * ZROWS, ZROWS), ZROWS)

    def x_copy(t, off):
        return remote(
            sx.at[t, off - 1], rx.at[t, off - 1], xsend.at[t, off - 1], xrecv.at[t, off - 1], xpeer(off)
        )

    def z_copy(t, off):
        return remote(
            sz.at[t, z_rows(off)], rz.at[t, off - 1], zsend.at[t, off - 1], zrecv.at[t, off - 1], zpeer(off)
        )

    def a_copy(t, off):
        mine = res_rows(0)
        return remote(
            res.at[t, mine], res.at[t, mine], asend.at[t, off - 1], arecv.at[t, off - 1], zpeer(off)
        )

    def a_arrival(t, off):
        theirs = res_rows(NZ - off)
        return remote(
            res.at[t, theirs], res.at[t, theirs], asend.at[t, off - 1], arecv.at[t, off - 1], zpeer(off)
        )

    def b_copy(t, off):
        rows = chunk_rows(0)
        return remote(
            res.at[t, rows], res.at[t, rows], bsend.at[t, off - 1], brecv.at[t, off - 1], xpeer(off)
        )

    def b_arrival(t, off):
        rows = chunk_rows(NX - off)
        return remote(
            res.at[t, rows], res.at[t, rows], bsend.at[t, off - 1], brecv.at[t, off - 1], xpeer(off)
        )

    def reduce_partials(t, partial):
        for off in (2, 1, 3):
            sx[t, off - 1] = partial(off).astype(bf16)
            x_copy(t, off).start()
        xown[...] = partial(0)
        for off in (1, 3, 2):
            x_copy(t, off).wait_recv()
            xown[...] = xown[...] + rx[t, off - 1].astype(f32)
        sz[t] = xown[...].astype(bf16)

        def z_start(off, carry):
            z_copy(t, off).start()
            return carry

        lax.fori_loop(1, NZ, z_start, 0)

        def z_take(off, total):
            z_copy(t, off).wait_recv()
            return total + rz[t, off - 1].astype(f32)

        total = lax.fori_loop(1, NZ, z_take, xown[z_rows(0), :])
        res[t, res_rows(0), :] = total.astype(bf16)

        def a_start(off, carry):
            a_copy(t, off).start()
            return carry

        def a_take(off, carry):
            a_arrival(t, off).wait_recv()
            return carry

        lax.fori_loop(1, NZ, a_start, 0)
        lax.fori_loop(1, NZ, a_take, 0)
        for off in (2, 1, 3):
            b_copy(t, off).start()

    def structure(off):
        rows = chunk_rows(off)
        return both(cos_ref[rows, :], sin_ref[rows, :], False)

    reduce_partials(0, structure)

    force = jnp.zeros((8, ATOM), f32)
    for off in (0, 1, 3, 2):
        if off:
            b_arrival(0, off).wait_recv()
        rows = chunk_rows(NX - off)
        damp = wcol[rows, 3:4]
        coeff = res[0, rows, :]
        along_cos = nn(coeff, w1h[...]) + nn(coeff, w1l[...])
        along_sin = nn(coeff, w2h[...]) + nn(coeff, w2l[...])
        mixture = damp * (sin_ref[rows, :] * along_cos - cos_ref[rows, :] * along_sin)
        mh, ml = split(mixture)
        index = wpad[0:8, rows].astype(bf16)
        force = force + nn(index, mh) + nn(index, ml)
    pulls = []
    for a in range(3):
        row = force[a : a + 1, :] * steps[a]
        forces_ref[a : a + 1, :] = row
        pulls.append(2.0 * (row - fref_ref[a : a + 1, :]) * steps[a])

    dir_ref[...] = jnp.zeros_like(dir_ref)

    def gradient(off):
        rows = chunk_rows(off)
        cols = wcol[rows, :]
        slopes = cols[:, 0:1] * pulls[0] + cols[:, 1:2] * pulls[1] + cols[:, 2:3] * pulls[2]
        along_sin = slopes * sin_ref[rows, :]
        along_cos = slopes * cos_ref[rows, :]
        return along_sin, along_cos, cols[:, 3:4]

    def wave_term(off):
        along_sin, along_cos, damp = gradient(off)
        return both(along_sin, along_cos, True)

    reduce_partials(1, wave_term)

    for off in (0, 1, 3, 2):
        rows = chunk_rows(NX - off)
        along_sin, along_cos, damp = gradient(NX - off)
        coeff = res[0, rows, :].astype(f32).T.astype(bf16)
        sh, sl = split(damp * along_sin)
        ch, cl = split(damp * along_cos)
        direct = nn(coeff, sh) + nn(coeff, sl)
        minus = nn(coeff, ch) + nn(coeff, cl)
        dir_ref[...] = dir_ref[...] + (direct[0:CHARGES] - minus[CHARGES:CHAN])
        if off:
            b_arrival(1, off).wait_recv()
        back = res[1, rows, :].astype(f32).T.astype(bf16)
        ch, cl = split(damp * cos_ref[rows, :])
        sh, sl = split(damp * sin_ref[rows, :])
        first = nn(back, ch) + nn(back, cl)
        second = nn(back, sh) + nn(back, sl)
        dir_ref[...] = dir_ref[...] + (first[0:CHARGES] + second[CHARGES:CHAN])
    charge_grad = dir_ref[...]
    rounded = charge_grad.astype(bf16)
    pk[128:192, :] = nt(rounded, hidden_b)
    kinds = jnp.where(iota((8, ATOM), 0) == species, 1.0, 0.0).astype(bf16)
    gh, gl = split(charge_grad)
    pk[208:PACK, :] = jnp.zeros((PACK - 208, CHAN), f32)
    pk[208:216, 0:CHARGES] = nt(kinds, gh) + nt(kinds, gl)
    upstream = nn(cw_ref[...], rounded)
    before_grad = (upstream * slope).astype(bf16)
    pk[0:128, :] = nt(messages_b, before_grad)
    message_grad = nn(mw_ref[...], before_grad).astype(bf16).astype(f32)
    lane = iota((CHAN, CHAN), 1)
    radial_sum = jnp.zeros((CHAN, CHAN), f32)
    for b in range(BASIS):
        column = jnp.sum(message_grad * g_ref[b], axis=1, keepdims=True)
        radial_sum = jnp.where(lane == b, column, radial_sum)
    pk[192:208, :] = radial_sum.T[0:BASIS, :]

    def p_rows(off):
        return pl.ds(pl.multiple_of(zat(off) * PROWS, PROWS), PROWS)

    def z3_copy(off):
        return remote(sg.at[p_rows(off)], rz3.at[off - 1], z3send.at[off - 1], z3recv.at[off - 1], zpeer(off))

    def x3_copy(off):
        return remote(xb3.at[xi], xb3.at[xi], x3send.at[off - 1], x3recv.at[off - 1], xpeer(off))

    def x3_arrival(off):
        theirs = lax.rem(xi + NX - off, NX)
        return remote(xb3.at[theirs], xb3.at[theirs], x3send.at[off - 1], x3recv.at[off - 1], xpeer(off))

    def a3_copy(off):
        mine = p_rows(0)
        return remote(res3.at[mine], res3.at[mine], a3send.at[off - 1], a3recv.at[off - 1], zpeer(off))

    def a3_arrival(off):
        theirs = p_rows(NZ - off)
        return remote(res3.at[theirs], res3.at[theirs], a3send.at[off - 1], a3recv.at[off - 1], zpeer(off))

    sg[...] = pk[...].astype(bf16)

    def z3_start(off, carry):
        z3_copy(off).start()
        return carry

    def z3_take(off, total):
        z3_copy(off).wait_recv()
        return total + rz3[off - 1].astype(f32)

    lax.fori_loop(1, NZ, z3_start, 0)
    xb3[xi] = lax.fori_loop(1, NZ, z3_take, pk[p_rows(0), :])
    for off in (2, 1, 3):
        x3_copy(off).start()
    for off in (1, 3, 2):
        x3_arrival(off).wait_recv()
    res3[p_rows(0), :] = (xb3[0] + xb3[1] + xb3[2] + xb3[3]).astype(bf16)

    def a3_start(off, carry):
        a3_copy(off).start()
        return carry

    def a3_take(off, carry):
        a3_arrival(off).wait_recv()
        return carry

    lax.fori_loop(1, NZ, a3_start, 0)
    lax.fori_loop(1, NZ, a3_take, 0)

    def scaled(value, count):
        return value / jnp.sqrt(sum_all(value * value) * (1.0 / count) + 1e-06)

    mstep_ref[...] = scaled(res3[0:128, :].astype(f32), CHAN * CHAN)
    tpad[...] = jnp.zeros_like(tpad)
    tpad[0:CHARGES, :] = scaled(res3[128:192, :].astype(f32), CHAN * CHARGES)
    cstep_ref[...] = tpad[...].T[:, 0:CHARGES]
    rstep_ref[...] = scaled(res3[192:208, :].astype(f32), BASIS * CHAN)
    tail = scaled(res3[208:224, :].astype(f32), SPECIES * CHARGES)
    sstep_ref[...] = tail[0:SPECIES, 0:CHARGES]

    for copy in ghost_copies:
        copy.wait_send()
    for t in range(2):
        for off in range(1, NX):
            x_copy(t, off).wait_send()
            b_copy(t, off).wait_send()
    for off in range(1, NX):
        x3_copy(off).wait_send()

    def drain(off, carry):
        for t in range(2):
            z_copy(t, off).wait_send()
            a_copy(t, off).wait_send()
        z3_copy(off).wait_send()
        a3_copy(off).wait_send()
        return carry

    lax.fori_loop(1, NZ, drain, 0)


def on_device(
    features, positions, neighbours, neighbour_count, ghost_sends, species,
    wave_index, force_ref, radial_weight, mix_weight, charge_weight, species_charge,
):
    dma = pltpu.SemaphoreType.DMA
    vmem = pltpu.VMEM
    wide = [vmem((CHAN, ATOM), bf16)] * 4 + [vmem((ATOM, CHAN), bf16)] * 4
    scratch = [
        vmem((128, WAVES), f32),
        vmem((WAVES, 128), f32),
        vmem((128, ATOM), f32),
        vmem((TABLE, 128), f32),
        vmem((128, 128), f32),
        vmem((WAVES, ATOM), f32),
        vmem((WAVES, ATOM), f32),
        vmem((SLOTS, ATOM), jnp.int32),
        vmem((SLOTS, ATOM), jnp.int32),
        vmem((TABLE // 32, ATOM), jnp.int32),
        vmem((BASIS, TABLE, ATOM), bf16),
        vmem((BASIS, TABLE, ATOM), bf16),
        vmem((BASIS, CHAN, ATOM), f32),
        vmem((2, CHAN, ATOM), bf16),
        vmem((2, 8, ATOM), f32),
        vmem((2, CHAN, ATOM), bf16),
        vmem((2, 8, ATOM), f32),
        *wide,
        vmem((8, ATOM), f32),
        vmem((CHARGES, ATOM), f32),
        vmem((2, NX - 1, XROWS, CHAN), bf16),
        vmem((2, NX - 1, XROWS, CHAN), bf16),
        vmem((XROWS, CHAN), f32),
        vmem((2, XROWS, CHAN), bf16),
        vmem((2, NZ - 1, ZROWS, CHAN), bf16),
        vmem((2, WAVES, CHAN), bf16),
        vmem((PACK, CHAN), bf16),
        vmem((PACK, CHAN), f32),
        vmem((NZ - 1, PROWS, CHAN), bf16),
        vmem((NX, PROWS, CHAN), f32),
        vmem((PACK, CHAN), bf16),
        dma((4,)),
        dma((4,)),
        dma((2, NX - 1)),
        dma((2, NX - 1)),
        dma((2, NZ - 1)),
        dma((2, NZ - 1)),
        dma((2, NZ - 1)),
        dma((2, NZ - 1)),
        dma((2, NX - 1)),
        dma((2, NX - 1)),
        dma((NZ - 1,)),
        dma((NZ - 1,)),
        dma((NX - 1,)),
        dma((NX - 1,)),
        dma((NZ - 1,)),
        dma((NZ - 1,)),
    ]
    spec = pl.BlockSpec(memory_space=pltpu.VMEM)
    return pl.pallas_call(
        kernel,
        out_shape=(
            jax.ShapeDtypeStruct((3, ATOM), f32),
            jax.ShapeDtypeStruct((BASIS, CHAN), f32),
            jax.ShapeDtypeStruct((CHAN, CHAN), f32),
            jax.ShapeDtypeStruct((CHAN, CHARGES), f32),
            jax.ShapeDtypeStruct((SPECIES, CHARGES), f32),
        ),
        in_specs=[spec] * 12,
        out_specs=(spec,) * 5,
        scratch_shapes=scratch,
        compiler_params=pltpu.CompilerParams(
            collective_id=0, has_side_effects=True, vmem_limit_bytes=48 * 1024 * 1024
        ),
        name="step",
    )(
        features,
        positions,
        neighbours,
        neighbour_count.reshape(1, ATOM),
        ghost_sends,
        species.reshape(1, ATOM),
        wave_index,
        force_ref,
        radial_weight,
        mix_weight,
        charge_weight,
        species_charge,
    )


def solution(mesh):
    placed = (
        P(("cell", "dom"), None),
        P(None, ("cell", "dom")),
        P(("cell", "dom"), None),
        P(("cell", "dom")),
        P(None, ("cell", "dom")),
        P(("cell", "dom")),
        P(),
        P(None, ("cell", "dom")),
        P(),
        P(),
        P(),
        P(),
    )
    return jax.shard_map(
        on_device,
        mesh=mesh,
        in_specs=placed,
        out_specs=(
            P(None, ("cell", "dom")),
            P("cell", None),
            P("cell", None),
            P("cell", None),
            P("cell", None),
        ),
        check_vma=False,
    )
```

```python
import math

import jax
import jax.numpy as jnp
from jax import lax
from jax.experimental import pallas as pl
from jax.experimental.pallas import tpu as pltpu
from jax.sharding import PartitionSpec as P

f32 = jnp.float32
bf16 = jnp.bfloat16
MESH = pl.DeviceIdType.MESH

ATOM = 256
CHAN = 128
CHARGES = 64
WAVES = 1024
SLOTS = 64
BASIS = 16
SPECIES = 6
TABLE = 3 * ATOM
NX = 4
NZ = 16
DOMS = NX * NZ
TOTAL = ATOM * DOMS
XROWS = WAVES // NX
ZROWS = XROWS // NZ
PACK = 256
PROWS = PACK // NZ
SIDES = (1.25 * TOTAL / 64, 20.0, 20.0)
CUTOFF = 5.0
SPREAD = 2.0 * math.sqrt(math.log2(math.e))
CENTERS = [0.5 + 4.5 * b / 15 for b in range(BASIS)]
COS_QUARTER = [(-1.0) ** n * (math.pi / 2) ** (2 * n) / math.factorial(2 * n) for n in range(8)]
SIN_HALF = [(-1.0) ** n * math.pi ** (2 * n + 1) / math.factorial(2 * n + 1) for n in range(8)]
COS_HALF = [(-1.0) ** n * math.pi ** (2 * n) / math.factorial(2 * n) for n in range(9)]


def nn(left, right):
    return lax.dot_general(left, right, (((1,), (0,)), ((), ())), preferred_element_type=f32)


def nt(left, right):
    return lax.dot_general(left, right, (((1,), (1,)), ((), ())), preferred_element_type=f32)


def split(value):
    high = value.astype(bf16)
    return high, (value - high.astype(f32)).astype(bf16)


def poly(coeffs, square):
    total = jnp.full_like(square, coeffs[-1])
    for coeff in reversed(coeffs[:-1]):
        total = total * square + coeff
    return total


def iota(shape, dim):
    return lax.broadcasted_iota(jnp.int32, shape, dim)


def sum_all(value):
    return jnp.sum(jnp.sum(value, axis=1, keepdims=True), axis=0, keepdims=True)


def kernel(
    feat_ref, pos_ref, nbr_ref, cnt_ref, ghost_ref, spec_ref, wave_ref, fref_ref,
    rw_ref, mw_ref, cwt_ref, sc_ref,
    forces_ref, total_ref,
    wpad, wcol, kb, ppad, pcol, tpad, cos_ref, sin_ref, ch_ref, cl_ref, sh_ref, sl_ref,
    ssh_ref, ssl_ref, sch_ref, scl_ref, idx_ref, bit_ref, word_ref,
    m_ref, ml_ref, g_ref, outf, outp, gf, gp,
    xpos, qall, tq, fsend, frecv, cg_ref, cgs, cgr,
    wave32, sz, rz, res, sg, pk, rz3, xb3, res3,
    gsend, grecv, psend, precv, qsend, qrecv, fsem, frsem, csend, crecv,
    zsend, zrecv, asend, arecv, z3send, z3recv, x3send, x3recv, a3send, a3recv,
):
    me = lax.axis_index("dom")
    xi = lax.div(me, NZ)
    zi = lax.rem(me, NZ)
    upper = lax.rem(me + 1, DOMS)
    lower = lax.rem(me + DOMS - 1, DOMS)

    def xpeer(off):
        return lax.rem(xi + off, NX) * NZ + zi

    def zat(off):
        return lax.rem(zi + off, NZ)

    def far_first(step):
        return NZ // 2 + (1 - 2 * lax.rem(step, 2)) * lax.div(step + 1, 2)

    def zpeer(off):
        return xi * NZ + zat(off)

    barrier = pltpu.get_barrier_semaphore()

    def greet(target):
        pl.semaphore_signal(barrier, inc=1, device_id={"dom": target}, device_id_type=MESH)

    def greet_z(step, carry):
        greet(zpeer(far_first(step)))
        return carry

    lax.fori_loop(0, NZ - 1, greet_z, 0)
    for off in range(1, NX):
        greet(xpeer(off))
    greet(upper)
    greet(lower)

    def remote(src, dst, send, recv, target):
        return pltpu.make_async_remote_copy(
            src_ref=src, dst_ref=dst, send_sem=send, recv_sem=recv,
            device_id={"dom": target}, device_id_type=MESH,
        )

    ft32 = feat_ref[...].astype(f32).T
    ftb = ft32.astype(bf16)
    tpad[...] = jnp.zeros_like(tpad)
    ppad[...] = jnp.zeros_like(ppad)
    ppad[0:3, :] = pos_ref[...]
    own8 = ppad[0:8, :]
    pcol[0:ATOM, :] = ppad[...].T
    p1 = own8.astype(bf16)
    p2 = (own8 - p1.astype(f32)).astype(bf16)
    p3 = (own8 - p1.astype(f32) - p2.astype(f32)).astype(bf16)
    rows_of = iota((ATOM, ATOM), 0)
    for r in range(2):
        perm = jnp.where(rows_of == ghost_ref[r : r + 1, :], 1.0, 0.0).astype(bf16)
        outf[r] = nn(ftb, perm).astype(bf16)
        outp[r] = nn(p1, perm) + nn(p2, perm) + nn(p3, perm)
    xpos[0] = own8
    xpos[0, 3:6, :] = fref_ref[...]

    wave = wave_ref[...].astype(f32)
    wpad[...] = jnp.zeros_like(wpad)
    wpad[0:3, :] = wave
    steps = [2.0 * math.pi / side for side in SIDES]
    square = sum((wave[a : a + 1, :] * steps[a]) ** 2 for a in range(3))
    wpad[3:4, :] = jnp.exp(-0.5 * square) * (1.0 / TOTAL)
    mine = pl.ds(pl.multiple_of(xi * XROWS, XROWS), XROWS)
    wcol[...] = wpad[:, mine].T
    damp_col = jnp.broadcast_to(wcol[:, 3:4], (XROWS, 128))
    kb[3] = damp_col
    for a in range(3):
        spread = jnp.broadcast_to(wcol[:, a : a + 1], (XROWS, 128))
        kb[a] = spread
        kb[4 + a] = spread * damp_col

    def twice(value):
        return jnp.concatenate([value, value], axis=1)

    def phases(block):
        own = xpos[block]
        tx, ty, tz = (own[a : a + 1, :] * (1.0 / SIDES[a]) for a in range(3))

        def phase_block(step, carry):
            rows = pl.ds(pl.multiple_of(step * 32, 32), 32)
            turns = (
                twice(kb[0, rows, :]) * tx + twice(kb[1, rows, :]) * ty + twice(kb[2, rows, :]) * tz
            )
            turns = turns - jnp.floor(turns + 0.5)
            sq = turns * turns
            half_sin = turns * poly(SIN_HALF, sq)
            half_cos = poly(COS_HALF, sq)
            cosine = 1.0 - 2.0 * half_sin * half_sin
            sine = 2.0 * half_sin * half_cos
            cos_ref[block, rows, :] = cosine
            sin_ref[block, rows, :] = sine
            ch_ref[block, rows, :], cl_ref[block, rows, :] = split(cosine)
            sh_ref[block, rows, :], sl_ref[block, rows, :] = split(sine)
            return carry

        lax.fori_loop(0, XROWS // 32, phase_block, 0)

    phases(0)

    entries = nbr_ref[...]
    live = iota((SLOTS, ATOM), 0) < cnt_ref[...]
    idx_ref[...] = jnp.where(live, lax.shift_right_logical(entries, 5), -1)
    bit_ref[...] = lax.shift_left(jnp.ones_like(entries), entries & 31)
    word_rows = iota((TABLE // 32, ATOM), 0)

    def word_step(n, words):
        hit = word_rows == idx_ref[pl.ds(n, 1), :]
        return words | jnp.where(hit, bit_ref[pl.ds(n, 1), :], 0)

    word_ref[...] = lax.fori_loop(
        0, SLOTS, word_step, jnp.zeros((TABLE // 32, ATOM), jnp.int32)
    )

    pl.semaphore_wait(barrier, NZ - 1 + NX - 1 + 2)

    ghost_copies = []
    for r, target in ((1, upper), (0, lower)):
        slot = 1 - r
        ghost_copies.append(
            remote(outp.at[r], gp.at[slot], gsend.at[2 * slot], grecv.at[2 * slot], target)
        )
        ghost_copies.append(
            remote(outf.at[r], gf.at[slot], gsend.at[2 * slot + 1], grecv.at[2 * slot + 1], target)
        )

    def x_message(src, dst_ref, send, recv, off):
        return remote(src, dst_ref.at[off], send.at[off - 1], recv.at[off - 1], xpeer(off))

    for copy in ghost_copies:
        copy.start()
    pos_copies = {off: x_message(xpos.at[0], xpos, psend, precv, off) for off in (2, 1, 3)}
    for copy in pos_copies.values():
        copy.start()

    px, py, pz = (pos_ref[a : a + 1, :] for a in range(3))
    shifts = iota((32, ATOM), 0)

    def edge_block(step, carry):
        rows = pl.ds(pl.multiple_of(step * 32, 32), 32)
        cols = pcol[rows, :]
        dist2 = jnp.zeros((32, ATOM), f32)
        for a, own in enumerate((px, py, pz)):
            delta = cols[:, a : a + 1] - own
            delta = delta - SIDES[a] * jnp.floor(delta * (1.0 / SIDES[a]) + 0.5)
            dist2 = dist2 + delta * delta
        dist = jnp.sqrt(dist2)
        part = jnp.minimum(dist, CUTOFF) * (1.0 / CUTOFF)
        fade = poly(COS_QUARTER, part * part)
        mask = lax.shift_right_logical(
            jnp.broadcast_to(word_ref[pl.ds(step, 1), :], (32, ATOM)), shifts
        ) & 1
        weight = fade * fade * mask.astype(f32)
        scaled = dist * SPREAD
        for b in range(BASIS):
            away = scaled - SPREAD * CENTERS[b]
            basis = jnp.exp2(-(away * away)).astype(bf16)
            m_ref[b, rows, :], ml_ref[b, rows, :] = split(basis.astype(f32) * weight)
        return carry

    lax.fori_loop(0, ATOM // 32, edge_block, 0)
    for b in range(BASIS):
        g_ref[b] = nn(ftb, m_ref[b, 0:ATOM, :]) + nn(ftb, ml_ref[b, 0:ATOM, :])

    for copy in ghost_copies:
        copy.wait_recv()
    for slot in range(2):
        ppad[0:8, :] = gp[slot]
        pcol[(1 + slot) * ATOM : (2 + slot) * ATOM, :] = ppad[...].T
    lax.fori_loop(ATOM // 32, TABLE // 32, edge_block, 0)

    tpad[0:BASIS, :] = rw_ref[...].astype(f32)
    radial = tpad[...].T
    messages = jnp.zeros((CHAN, ATOM), f32)
    for b in range(BASIS):
        gathered = g_ref[b]
        for part in (m_ref, ml_ref):
            gathered = (
                gathered
                + nn(gf[0], part[b, ATOM : 2 * ATOM, :])
                + nn(gf[1], part[b, 2 * ATOM : TABLE, :])
            )
        g_ref[b] = gathered
        messages = messages + radial[:, b : b + 1] * gathered
    messages_b = messages.astype(bf16)
    mixT = mw_ref[...].astype(f32).T.astype(bf16)
    before = nn(mixT, messages_b)
    sigmoid = 1.0 / (1.0 + jnp.exp(-before))
    hidden_b = (ft32 + before * sigmoid).astype(bf16)
    slope = sigmoid * (1.0 + before * (1.0 - sigmoid))
    cwT = cwt_ref[...]
    tpad[0:CHARGES, :] = cwT.astype(f32)
    cw = tpad[...].T[:, 0:CHARGES].astype(bf16)
    tpad[...] = jnp.zeros_like(tpad)
    tpad[0:SPECIES, 0:CHARGES] = sc_ref[...]
    offsets = tpad[...].T[0:CHARGES, :]
    species = spec_ref[...]
    charges = nn(cwT, hidden_b)
    added = jnp.zeros((CHARGES, ATOM), f32)
    for s in range(SPECIES):
        added = jnp.where(species == s, offsets[:, s : s + 1], added)
    qall[0, 0:CHARGES, :], qall[0, CHARGES:CHAN, :] = split(charges + added)
    charge_copies = {off: x_message(qall.at[0], qall, qsend, qrecv, off) for off in (2, 1, 3)}
    for copy in charge_copies.values():
        copy.start()

    for off in (1, 3, 2):
        pos_copies[off].wait_recv()
        phases(off)

    lane = iota((XROWS, CHAN), 1)

    def fold(one, two):
        one = one + pltpu.roll(one, CHARGES, 1)
        two = two + pltpu.roll(two, CHARGES, 1)
        return jnp.where(lane < CHARGES, one, two)

    def z_rows(off):
        return pl.ds(pl.multiple_of(zat(off) * ZROWS, ZROWS), ZROWS)

    def z_copy(t, off):
        return remote(
            sz.at[t, z_rows(off)], rz.at[t, off - 1], zsend.at[t, off - 1], zrecv.at[t, off - 1], zpeer(off)
        )

    def a_copy(t, off):
        rows = z_rows(0)
        return remote(
            res.at[t, rows], res.at[t, rows], asend.at[t, off - 1], arecv.at[t, off - 1], zpeer(off)
        )

    def a_arrival(t, off):
        rows = z_rows(NZ - off)
        return remote(
            res.at[t, rows], res.at[t, rows], asend.at[t, off - 1], arecv.at[t, off - 1], zpeer(off)
        )

    def reduce_start(t, partial):
        wave32[...] = partial
        sz[t] = partial.astype(bf16)

        def z_start(step, carry):
            z_copy(t, far_first(step)).start()
            return carry

        lax.fori_loop(0, NZ - 1, z_start, 0)

    def reduce_finish(t):
        def z_take(step, total):
            off = far_first(NZ - 2 - step)
            z_copy(t, off).wait_recv()
            return total + rz[t, off - 1].astype(f32)

        total = lax.fori_loop(0, NZ - 1, z_take, wave32[z_rows(0), :])
        res[t, z_rows(0), :] = total.astype(bf16)

        def a_start(step, carry):
            a_copy(t, far_first(step)).start()
            return carry

        lax.fori_loop(0, NZ - 1, a_start, 0)

    def gather_finish(t):
        def a_take(step, carry):
            a_arrival(t, far_first(NZ - 2 - step)).wait_recv()
            return carry

        lax.fori_loop(0, NZ - 1, a_take, 0)

    one = jnp.zeros((XROWS, CHAN), f32)
    two = jnp.zeros((XROWS, CHAN), f32)
    for s in (0, 1, 3, 2):
        if s:
            charge_copies[s].wait_recv()
        tq[s] = qall[s].astype(f32).T.astype(bf16)
        one = one + nn(ch_ref[s], tq[s]) + nn(cl_ref[s], tq[s])
        two = two + nn(sh_ref[s], tq[s]) + nn(sl_ref[s], tq[s])
    reduce_start(0, fold(one, two))
    reduce_finish(0)
    gather_finish(0)

    coeff = res[0].astype(f32)
    swapped = pltpu.roll(coeff, CHARGES, 1)
    cos_pair = jnp.where(lane < CHARGES, coeff, swapped).astype(bf16)
    sin_pair = jnp.where(lane < CHARGES, swapped, coeff).astype(bf16)

    def at_x(s):
        return lax.rem(xi + NX - s, NX)

    for s in range(NX):
        mixture = sin_ref[s] * nn(cos_pair, qall[s]) - cos_ref[s] * nn(sin_pair, qall[s])
        for a in range(3):
            row = jnp.sum(twice(kb[4 + a]) * mixture, axis=0, keepdims=True)
            fsend[pl.ds(a * NX + at_x(s), 1), :] = row
    force_copies = {
        off: remote(fsend, frecv.at[off - 1], fsem.at[off - 1], frsem.at[off - 1], xpeer(off))
        for off in (2, 1, 3)
    }
    for copy in force_copies.values():
        copy.start()

    def paired(value):
        high, low = split(value)
        first = jnp.concatenate([high[0:CHARGES], low[0:CHARGES]], axis=0)
        second = jnp.concatenate([high[CHARGES:CHAN], low[CHARGES:CHAN]], axis=0)
        return first, second

    coeff_cos, coeff_sin = paired((kb[3] * coeff).T)

    for off in (1, 3, 2):
        force_copies[off].wait_recv()
    pulls = []
    for s in range(NX):
        rows = []
        for a in range(3):
            at = pl.ds(a * NX + at_x(s), 1)
            row = fsend[at, :] + frecv[0, at, :] + frecv[1, at, :] + frecv[2, at, :]
            row = row * steps[a]
            if s == 0:
                forces_ref[a : a + 1, :] = row
            rows.append(2.0 * (row - xpos[s, 3 + a : 4 + a, :]) * steps[a])
        pulls.append(rows)

    one = jnp.zeros((XROWS, CHAN), f32)
    two = jnp.zeros((XROWS, CHAN), f32)
    for s in range(NX):
        slopes = (
            twice(kb[0]) * pulls[s][0] + twice(kb[1]) * pulls[s][1] + twice(kb[2]) * pulls[s][2]
        )
        ssh_ref[s], ssl_ref[s] = split(slopes * sin_ref[s])
        sch_ref[s], scl_ref[s] = split(slopes * cos_ref[s])
        one = one + nn(ssh_ref[s], tq[s]) + nn(ssl_ref[s], tq[s])
        two = two + nn(sch_ref[s], tq[s]) + nn(scl_ref[s], tq[s])
    reduce_start(1, fold(one, -two))

    for s in range(NX):
        direct = (
            nn(coeff_cos, ssh_ref[s]) + nn(coeff_cos, ssl_ref[s])
            - nn(coeff_sin, sch_ref[s]) - nn(coeff_sin, scl_ref[s])
        )
        cg_ref[s] = direct[0:CHARGES] + direct[CHARGES:CHAN]
    reduce_finish(1)
    gather_finish(1)
    back_cos, back_sin = paired((kb[3] * res[1].astype(f32)).T)

    def charge_part(s):
        back = (
            nn(back_cos, ch_ref[s]) + nn(back_cos, cl_ref[s])
            + nn(back_sin, sh_ref[s]) + nn(back_sin, sl_ref[s])
        )
        return cg_ref[s] + (back[0:CHARGES] + back[CHARGES:CHAN])

    owner_copies = {}
    for s in (2, 1, 3):
        cgs[s - 1] = charge_part(s).astype(bf16)
        owner_copies[s] = remote(
            cgs.at[s - 1], cgr.at[s - 1], csend.at[s - 1], crecv.at[s - 1], xpeer(NX - s)
        )
        owner_copies[s].start()
    charge_grad = charge_part(0)
    for s in (1, 3, 2):
        owner_copies[s].wait_recv()
        charge_grad = charge_grad + cgr[s - 1].astype(f32)

    rounded = charge_grad.astype(bf16)
    pk[128:192, :] = nt(rounded, hidden_b)
    kinds = jnp.where(iota((8, ATOM), 0) == species, 1.0, 0.0).astype(bf16)
    gh, gl = split(charge_grad)
    pk[208:PACK, :] = jnp.zeros((PACK - 208, CHAN), f32)
    pk[208:216, 0:CHARGES] = nt(kinds, gh) + nt(kinds, gl)
    upstream = nn(cw, rounded)
    before_grad = (upstream * slope).astype(bf16)
    pk[0:128, :] = nt(messages_b, before_grad)
    message_grad = nn(mw_ref[...], before_grad).astype(bf16).astype(f32)
    lanes = iota((CHAN, CHAN), 1)
    radial_sum = jnp.zeros((CHAN, CHAN), f32)
    for b in range(BASIS):
        column = jnp.sum(message_grad * g_ref[b], axis=1, keepdims=True)
        radial_sum = jnp.where(lanes == b, column, radial_sum)
    pk[192:208, :] = radial_sum.T[0:BASIS, :]

    def p_rows(off):
        return pl.ds(pl.multiple_of(zat(off) * PROWS, PROWS), PROWS)

    def z3_copy(off):
        return remote(sg.at[p_rows(off)], rz3.at[off - 1], z3send.at[off - 1], z3recv.at[off - 1], zpeer(off))

    def x3_copy(off):
        return remote(xb3.at[xi], xb3.at[xi], x3send.at[off - 1], x3recv.at[off - 1], xpeer(off))

    def x3_arrival(off):
        theirs = lax.rem(xi + NX - off, NX)
        return remote(xb3.at[theirs], xb3.at[theirs], x3send.at[off - 1], x3recv.at[off - 1], xpeer(off))

    def a3_copy(off):
        mine = p_rows(0)
        return remote(res3.at[mine], res3.at[mine], a3send.at[off - 1], a3recv.at[off - 1], zpeer(off))

    def a3_arrival(off):
        theirs = p_rows(NZ - off)
        return remote(res3.at[theirs], res3.at[theirs], a3send.at[off - 1], a3recv.at[off - 1], zpeer(off))

    sg[...] = pk[...].astype(bf16)

    def z3_start(step, carry):
        z3_copy(far_first(step)).start()
        return carry

    def z3_take(step, total):
        off = far_first(NZ - 2 - step)
        z3_copy(off).wait_recv()
        return total + rz3[off - 1].astype(f32)

    lax.fori_loop(0, NZ - 1, z3_start, 0)
    xb3[xi] = lax.fori_loop(0, NZ - 1, z3_take, pk[p_rows(0), :])
    for off in (2, 1, 3):
        x3_copy(off).start()
    for off in (1, 3, 2):
        x3_arrival(off).wait_recv()
    res3[p_rows(0), :] = (xb3[0] + xb3[1] + xb3[2] + xb3[3]).astype(bf16)

    def a3_start(step, carry):
        a3_copy(far_first(step)).start()
        return carry

    def a3_take(step, carry):
        a3_arrival(far_first(NZ - 2 - step)).wait_recv()
        return carry

    lax.fori_loop(0, NZ - 1, a3_start, 0)
    lax.fori_loop(0, NZ - 1, a3_take, 0)

    total_ref[...] = res3[...]

    for copy in ghost_copies:
        copy.wait_send()
    for copies in (pos_copies, charge_copies, force_copies, owner_copies):
        for copy in copies.values():
            copy.wait_send()
    for off in range(1, NX):
        x3_copy(off).wait_send()

    def drain(off, carry):
        for t in range(2):
            z_copy(t, off).wait_send()
            a_copy(t, off).wait_send()
        z3_copy(off).wait_send()
        a3_copy(off).wait_send()
        return carry

    lax.fori_loop(1, NZ, drain, 0)


def finish(
    raw_ref, total_ref, forces_ref, rstep_ref, mstep_ref, cstep_ref, sstep_ref
):
    def scaled(rows, count):
        value = total_ref[rows, :].astype(f32)
        return value / jnp.sqrt(sum_all(value * value) * (1.0 / count) + 1e-06)

    forces_ref[...] = raw_ref[...]
    mstep_ref[...] = scaled(slice(0, 128), CHAN * CHAN)
    cstep_ref[...] = scaled(slice(128, 192), CHAN * CHARGES)
    rstep_ref[...] = scaled(slice(192, 208), BASIS * CHAN)
    sstep_ref[...] = scaled(slice(208, 224), SPECIES * CHARGES)[0:SPECIES, 0:CHARGES]


def on_device(
    features, positions, neighbours, neighbour_count, ghost_sends, species,
    wave_index, force_ref, radial_weight, mix_weight, charge_weight, species_charge,
):
    dma = pltpu.SemaphoreType.DMA
    vmem = pltpu.VMEM
    scratch = [
        vmem((128, WAVES), f32),
        vmem((XROWS, 128), f32),
        vmem((7, XROWS, 128), f32),
        vmem((128, ATOM), f32),
        vmem((TABLE, 128), f32),
        vmem((128, 128), f32),
        *[vmem((NX, XROWS, ATOM), f32)] * 2,
        *[vmem((NX, XROWS, ATOM), bf16)] * 8,
        vmem((SLOTS, ATOM), jnp.int32),
        vmem((SLOTS, ATOM), jnp.int32),
        vmem((TABLE // 32, ATOM), jnp.int32),
        vmem((BASIS, TABLE, ATOM), bf16),
        vmem((BASIS, TABLE, ATOM), bf16),
        vmem((BASIS, CHAN, ATOM), f32),
        vmem((2, CHAN, ATOM), bf16),
        vmem((2, 8, ATOM), f32),
        vmem((2, CHAN, ATOM), bf16),
        vmem((2, 8, ATOM), f32),
        vmem((NX, 8, ATOM), f32),
        vmem((NX, CHAN, ATOM), bf16),
        vmem((NX, ATOM, CHAN), bf16),
        vmem((16, ATOM), f32),
        vmem((NX - 1, 16, ATOM), f32),
        vmem((NX, CHARGES, ATOM), f32),
        vmem((NX - 1, CHARGES, ATOM), bf16),
        vmem((NX - 1, CHARGES, ATOM), bf16),
        vmem((XROWS, CHAN), f32),
        vmem((2, XROWS, CHAN), bf16),
        vmem((2, NZ - 1, ZROWS, CHAN), bf16),
        vmem((2, XROWS, CHAN), bf16),
        vmem((PACK, CHAN), bf16),
        vmem((PACK, CHAN), f32),
        vmem((NZ - 1, PROWS, CHAN), bf16),
        vmem((NX, PROWS, CHAN), f32),
        vmem((PACK, CHAN), bf16),
        dma((4,)),
        dma((4,)),
        *[dma((NX - 1,))] * 8,
        *[dma((2, NZ - 1))] * 4,
        dma((NZ - 1,)),
        dma((NZ - 1,)),
        dma((NX - 1,)),
        dma((NX - 1,)),
        dma((NZ - 1,)),
        dma((NZ - 1,)),
    ]
    spec = pl.BlockSpec(memory_space=pltpu.VMEM)
    raw, total = pl.pallas_call(
        kernel,
        out_shape=(
            jax.ShapeDtypeStruct((3, ATOM), f32),
            jax.ShapeDtypeStruct((PACK, CHAN), bf16),
        ),
        in_specs=[spec] * 12,
        out_specs=(spec,) * 2,
        scratch_shapes=scratch,
        compiler_params=pltpu.CompilerParams(
            collective_id=0, has_side_effects=True, vmem_limit_bytes=48 * 1024 * 1024
        ),
        name="step",
    )(
        features,
        positions,
        neighbours.T,
        neighbour_count.reshape(1, ATOM),
        ghost_sends,
        species.reshape(1, ATOM),
        wave_index,
        force_ref,
        radial_weight,
        mix_weight,
        charge_weight.T,
        species_charge,
    )
    forces, rstep, mstep, cstep, sstep = pl.pallas_call(
        finish,
        out_shape=(
            jax.ShapeDtypeStruct((3, ATOM), f32),
            jax.ShapeDtypeStruct((BASIS, CHAN), f32),
            jax.ShapeDtypeStruct((CHAN, CHAN), f32),
            jax.ShapeDtypeStruct((CHARGES, CHAN), f32),
            jax.ShapeDtypeStruct((SPECIES, CHARGES), f32),
        ),
        in_specs=[spec] * 2,
        out_specs=(spec,) * 5,
        name="finish",
    )(raw, total)
    return forces, rstep, mstep, cstep.T, sstep


def solution(mesh):
    placed = (
        P(("cell", "dom"), None),
        P(None, ("cell", "dom")),
        P(("cell", "dom"), None),
        P(("cell", "dom")),
        P(None, ("cell", "dom")),
        P(("cell", "dom")),
        P(),
        P(None, ("cell", "dom")),
        P(),
        P(),
        P(),
        P(),
    )
    return jax.shard_map(
        on_device,
        mesh=mesh,
        in_specs=placed,
        out_specs=(
            P(None, ("cell", "dom")),
            P("cell", None),
            P("cell", None),
            P("cell", None),
            P("cell", None),
        ),
        check_vma=False,
    )
```

```python
import math

import jax
import jax.numpy as jnp
from jax import lax
from jax.experimental import pallas as pl
from jax.experimental.pallas import tpu as pltpu
from jax.sharding import PartitionSpec as P

f32 = jnp.float32
bf16 = jnp.bfloat16
MESH = pl.DeviceIdType.MESH

ATOM = 256
CHAN = 128
CHARGES = 64
WAVES = 1024
SLOTS = 64
BASIS = 16
SPECIES = 6
TABLE = 3 * ATOM
NX = 4
NZ = 16
DOMS = NX * NZ
TOTAL = ATOM * DOMS
XROWS = WAVES // NX
ZROWS = XROWS // NZ
PACK = 256
PROWS = PACK // NZ
SIDES = (1.25 * TOTAL / 64, 20.0, 20.0)
CUTOFF = 5.0
SPREAD = 2.0 * math.sqrt(math.log2(math.e))
CENTERS = [0.5 + 4.5 * b / 15 for b in range(BASIS)]
COS_QUARTER = [(-1.0) ** n * (math.pi / 2) ** (2 * n) / math.factorial(2 * n) for n in range(8)]
SIN_HALF = [(-1.0) ** n * math.pi ** (2 * n + 1) / math.factorial(2 * n + 1) for n in range(8)]
COS_HALF = [(-1.0) ** n * math.pi ** (2 * n) / math.factorial(2 * n) for n in range(9)]


def nn(left, right):
    return lax.dot_general(left, right, (((1,), (0,)), ((), ())), preferred_element_type=f32)


def nt(left, right):
    return lax.dot_general(left, right, (((1,), (1,)), ((), ())), preferred_element_type=f32)


def split(value):
    high = value.astype(bf16)
    return high, (value - high.astype(f32)).astype(bf16)


def poly(coeffs, square):
    total = jnp.full_like(square, coeffs[-1])
    for coeff in reversed(coeffs[:-1]):
        total = total * square + coeff
    return total


def iota(shape, dim):
    return lax.broadcasted_iota(jnp.int32, shape, dim)


def sum_all(value):
    return jnp.sum(jnp.sum(value, axis=1, keepdims=True), axis=0, keepdims=True)


def kernel(
    feat_in, pos_in, nbr_in, cnt_in, ghost_in, spec_in, wave_in, fref_in,
    rw_in, mw_in, cwt_in, sc_in,
    forces_ref, total_ref,
    feat_ref, pos_ref, nbr_ref, cnt_ref, ghost_ref, spec_ref, wave_ref, fref_ref,
    rw_ref, mw_ref, cwt_ref, sc_ref, in_sem,
    wpad, wcol, kb, ppad, pcol, tpad, cos_ref, sin_ref, ch_ref, cl_ref, sh_ref, sl_ref,
    ssh_ref, ssl_ref, sch_ref, scl_ref, idx_ref, bit_ref, word_ref,
    weight_ref, scaled_ref, m_ref, ml_ref, g_ref, outf, outp, gf, gp,
    xpos, qall, tq, fsend, frecv, cg_ref, cgs, cgr,
    wave32, sz, rz, res, sg, pk, rz3, xb3, res3,
    rounds, gsend, grecv, psend, precv, qsend, qrecv, fsem, frsem, csend, crecv,
    zsend, zrecv, asend, arecv, z3send, z3recv, x3send, x3recv, a3send, a3recv,
):
    fetches = [
        pltpu.make_async_copy(src, dst, in_sem.at[i])
        for i, (src, dst) in enumerate((
            (feat_in, feat_ref), (pos_in, pos_ref), (ghost_in, ghost_ref), (fref_in, fref_ref),
            (wave_in, wave_ref), (nbr_in, nbr_ref), (cnt_in, cnt_ref), (rw_in, rw_ref),
            (mw_in, mw_ref), (cwt_in, cwt_ref), (sc_in, sc_ref), (spec_in, spec_ref),
        ))
    ]
    for copy in fetches:
        copy.start()
    me = lax.axis_index("dom")
    xi = lax.div(me, NZ)
    zi = lax.rem(me, NZ)
    upper = lax.rem(me + 1, DOMS)
    lower = lax.rem(me + DOMS - 1, DOMS)

    def xpeer(off):
        return lax.rem(xi + off, NX) * NZ + zi

    def zat(off):
        return lax.rem(zi + off, NZ)

    def far_first(step):
        return NZ // 2 + (1 - 2 * lax.rem(step, 2)) * lax.div(step + 1, 2)

    def zpeer(off):
        return xi * NZ + zat(off)

    barrier = pltpu.get_barrier_semaphore()

    def greet(target):
        pl.semaphore_signal(barrier, inc=1, device_id={"dom": target}, device_id_type=MESH)

    for off in range(1, NX):
        greet(xpeer(off))
    greet(upper)
    greet(lower)
    greet(zpeer(1))
    greet(zpeer(NZ - 1))

    def reach_tell(level):
        for off in (2**level, NZ - 2**level):
            pl.semaphore_signal(
                rounds.at[level], inc=1, device_id={"dom": zpeer(off)}, device_id_type=MESH
            )

    def reach_learn(level):
        pl.semaphore_wait(rounds.at[level], 2)

    def remote(src, dst, send, recv, target):
        return pltpu.make_async_remote_copy(
            src_ref=src, dst_ref=dst, send_sem=send, recv_sem=recv,
            device_id={"dom": target}, device_id_type=MESH,
        )

    for copy in fetches:
        copy.wait()

    ft32 = feat_ref[...].astype(f32).T
    ftb = ft32.astype(bf16)
    tpad[...] = jnp.zeros_like(tpad)
    ppad[...] = jnp.zeros_like(ppad)
    ppad[0:3, :] = pos_ref[...]
    own8 = ppad[0:8, :]
    pcol[0:ATOM, :] = ppad[...].T
    p1 = own8.astype(bf16)
    p2 = (own8 - p1.astype(f32)).astype(bf16)
    p3 = (own8 - p1.astype(f32) - p2.astype(f32)).astype(bf16)
    rows_of = iota((ATOM, ATOM), 0)
    for r in range(2):
        perm = jnp.where(rows_of == ghost_ref[r : r + 1, :], 1.0, 0.0).astype(bf16)
        outf[r] = nn(ftb, perm).astype(bf16)
        outp[r] = nn(p1, perm) + nn(p2, perm) + nn(p3, perm)
    xpos[0] = own8
    xpos[0, 3:6, :] = fref_ref[...]

    pl.semaphore_wait(barrier, NX - 1 + 4)

    ghost_copies = []
    for r, target in ((1, upper), (0, lower)):
        slot = 1 - r
        ghost_copies.append(
            remote(outp.at[r], gp.at[slot], gsend.at[2 * slot], grecv.at[2 * slot], target)
        )
        ghost_copies.append(
            remote(outf.at[r], gf.at[slot], gsend.at[2 * slot + 1], grecv.at[2 * slot + 1], target)
        )

    def x_message(src, dst_ref, send, recv, off):
        return remote(src, dst_ref.at[off], send.at[off - 1], recv.at[off - 1], xpeer(off))

    for copy in ghost_copies:
        copy.start()
    pos_copies = {off: x_message(xpos.at[0], xpos, psend, precv, off) for off in (2, 1, 3)}
    for copy in pos_copies.values():
        copy.start()

    reach_tell(0)

    wave = wave_ref[...].astype(f32)
    wpad[...] = jnp.zeros_like(wpad)
    wpad[0:3, :] = wave
    steps = [2.0 * math.pi / side for side in SIDES]
    square = sum((wave[a : a + 1, :] * steps[a]) ** 2 for a in range(3))
    wpad[3:4, :] = jnp.exp(-0.5 * square) * (1.0 / TOTAL)
    mine = pl.ds(pl.multiple_of(xi * XROWS, XROWS), XROWS)
    wcol[...] = wpad[:, mine].T
    damp_col = jnp.broadcast_to(wcol[:, 3:4], (XROWS, 128))
    kb[3] = damp_col
    for a in range(3):
        spread = jnp.broadcast_to(wcol[:, a : a + 1], (XROWS, 128))
        kb[a] = spread
        kb[4 + a] = spread * damp_col

    def twice(value):
        return jnp.concatenate([value, value], axis=1)

    def phases(block):
        own = xpos[block]
        tx, ty, tz = (own[a : a + 1, :] * (1.0 / SIDES[a]) for a in range(3))

        def phase_block(step, carry):
            rows = pl.ds(pl.multiple_of(step * 32, 32), 32)
            turns = (
                twice(kb[0, rows, :]) * tx + twice(kb[1, rows, :]) * ty + twice(kb[2, rows, :]) * tz
            )
            turns = turns - jnp.floor(turns + 0.5)
            sq = turns * turns
            half_sin = turns * poly(SIN_HALF, sq)
            half_cos = poly(COS_HALF, sq)
            cosine = 1.0 - 2.0 * half_sin * half_sin
            sine = 2.0 * half_sin * half_cos
            cos_ref[block, rows, :] = cosine
            sin_ref[block, rows, :] = sine
            ch_ref[block, rows, :], cl_ref[block, rows, :] = split(cosine)
            sh_ref[block, rows, :], sl_ref[block, rows, :] = split(sine)
            return carry

        lax.fori_loop(0, XROWS // 32, phase_block, 0)

    phases(0)

    entries = nbr_ref[...]
    live = iota((SLOTS, ATOM), 0) < cnt_ref[...]
    idx_ref[...] = jnp.where(live, lax.shift_right_logical(entries, 5), -1)
    bit_ref[...] = lax.shift_left(jnp.ones_like(entries), entries & 31)
    word_rows = iota((TABLE // 32, ATOM), 0)

    def word_step(n, words):
        hit = word_rows == idx_ref[pl.ds(n, 1), :]
        return words | jnp.where(hit, bit_ref[pl.ds(n, 1), :], 0)

    word_ref[...] = lax.fori_loop(
        0, SLOTS, word_step, jnp.zeros((TABLE // 32, ATOM), jnp.int32)
    )

    reach_learn(0)
    reach_tell(1)

    px, py, pz = (pos_ref[a : a + 1, :] for a in range(3))
    shifts = iota((32, ATOM), 0)

    def edge_block(step, carry):
        rows = pl.ds(pl.multiple_of(step * 32, 32), 32)
        cols = pcol[rows, :]
        dist2 = jnp.zeros((32, ATOM), f32)
        for a, own in enumerate((px, py, pz)):
            delta = cols[:, a : a + 1] - own
            delta = delta - SIDES[a] * jnp.floor(delta * (1.0 / SIDES[a]) + 0.5)
            dist2 = dist2 + delta * delta
        dist = jnp.sqrt(dist2)
        part = jnp.minimum(dist, CUTOFF) * (1.0 / CUTOFF)
        fade = poly(COS_QUARTER, part * part)
        mask = lax.shift_right_logical(
            jnp.broadcast_to(word_ref[pl.ds(step, 1), :], (32, ATOM)), shifts
        ) & 1
        weight_ref[rows, :] = fade * fade * mask.astype(f32)
        scaled_ref[rows, :] = dist * SPREAD
        return carry

    def edge_sums(block, feats):
        for b in range(BASIS):
            for start in range(0, ATOM, 32):
                at = pl.ds(block * ATOM + start, 32)
                away = scaled_ref[at, :] - SPREAD * CENTERS[b]
                basis = jnp.exp2(-(away * away)).astype(bf16).astype(f32)
                high, low = split(basis * weight_ref[at, :])
                m_ref[b, start : start + 32, :] = high
                ml_ref[b, start : start + 32, :] = low
            fresh = nn(feats, m_ref[b]) + nn(feats, ml_ref[b])
            g_ref[b] = fresh if block == 0 else g_ref[b] + fresh

    lax.fori_loop(0, ATOM // 32, edge_block, 0)
    edge_sums(0, ftb)
    reach_learn(1)
    reach_tell(2)

    for copy in ghost_copies:
        copy.wait_recv()
    for slot in range(2):
        ppad[0:8, :] = gp[slot]
        pcol[(1 + slot) * ATOM : (2 + slot) * ATOM, :] = ppad[...].T
    lax.fori_loop(ATOM // 32, TABLE // 32, edge_block, 0)
    edge_sums(1, gf[0])
    edge_sums(2, gf[1])

    tpad[0:BASIS, :] = rw_ref[...].astype(f32)
    radial = tpad[...].T
    messages = jnp.zeros((CHAN, ATOM), f32)
    for b in range(BASIS):
        messages = messages + radial[:, b : b + 1] * g_ref[b]
    messages_b = messages.astype(bf16)
    mixT = mw_ref[...].astype(f32).T.astype(bf16)
    before = nn(mixT, messages_b)
    sigmoid = 1.0 / (1.0 + jnp.exp(-before))
    hidden_b = (ft32 + before * sigmoid).astype(bf16)
    slope = sigmoid * (1.0 + before * (1.0 - sigmoid))
    cwT = cwt_ref[...]
    tpad[0:CHARGES, :] = cwT.astype(f32)
    cw = tpad[...].T[:, 0:CHARGES].astype(bf16)
    tpad[...] = jnp.zeros_like(tpad)
    tpad[0:SPECIES, 0:CHARGES] = sc_ref[...]
    offsets = tpad[...].T[0:CHARGES, :]
    species = spec_ref[...]
    charges = nn(cwT, hidden_b)
    added = jnp.zeros((CHARGES, ATOM), f32)
    for s in range(SPECIES):
        added = jnp.where(species == s, offsets[:, s : s + 1], added)
    qall[0, 0:CHARGES, :], qall[0, CHARGES:CHAN, :] = split(charges + added)
    charge_copies = {off: x_message(qall.at[0], qall, qsend, qrecv, off) for off in (2, 1, 3)}
    for copy in charge_copies.values():
        copy.start()

    for off in (1, 3, 2):
        pos_copies[off].wait_recv()
        phases(off)

    lane = iota((XROWS, CHAN), 1)

    def fold(one, two):
        one = one + pltpu.roll(one, CHARGES, 1)
        two = two + pltpu.roll(two, CHARGES, 1)
        return jnp.where(lane < CHARGES, one, two)

    def z_rows(off):
        return pl.ds(pl.multiple_of(zat(off) * ZROWS, ZROWS), ZROWS)

    def z_copy(t, off):
        return remote(
            sz.at[t, z_rows(off)], rz.at[t, off - 1], zsend.at[t, off - 1], zrecv.at[t, off - 1], zpeer(off)
        )

    def a_copy(t, off):
        rows = z_rows(0)
        return remote(
            res.at[t, rows], res.at[t, rows], asend.at[t, off - 1], arecv.at[t, off - 1], zpeer(off)
        )

    def a_arrival(t, off):
        rows = z_rows(NZ - off)
        return remote(
            res.at[t, rows], res.at[t, rows], asend.at[t, off - 1], arecv.at[t, off - 1], zpeer(off)
        )

    def reduce_start(t, partial):
        wave32[...] = partial
        sz[t] = partial.astype(bf16)

        def z_start(step, carry):
            z_copy(t, far_first(step)).start()
            return carry

        lax.fori_loop(0, NZ - 1, z_start, 0)

    def reduce_finish(t):
        def z_take(step, total):
            off = far_first(NZ - 2 - step)
            z_copy(t, off).wait_recv()
            return total + rz[t, off - 1].astype(f32)

        total = lax.fori_loop(0, NZ - 1, z_take, wave32[z_rows(0), :])
        res[t, z_rows(0), :] = total.astype(bf16)

        def a_start(step, carry):
            a_copy(t, far_first(step)).start()
            return carry

        lax.fori_loop(0, NZ - 1, a_start, 0)

    def gather_finish(t):
        def a_take(step, carry):
            a_arrival(t, far_first(NZ - 2 - step)).wait_recv()
            return carry

        lax.fori_loop(0, NZ - 1, a_take, 0)

    one = jnp.zeros((XROWS, CHAN), f32)
    two = jnp.zeros((XROWS, CHAN), f32)
    for s in (0, 1, 3, 2):
        if s:
            charge_copies[s].wait_recv()
        tq[s] = qall[s].astype(f32).T.astype(bf16)
        one = one + nn(ch_ref[s], tq[s]) + nn(cl_ref[s], tq[s])
        two = two + nn(sh_ref[s], tq[s]) + nn(sl_ref[s], tq[s])
    reach_learn(2)
    reduce_start(0, fold(one, two))
    reduce_finish(0)
    gather_finish(0)

    coeff = res[0].astype(f32)
    swapped = pltpu.roll(coeff, CHARGES, 1)
    cos_pair = jnp.where(lane < CHARGES, coeff, swapped).astype(bf16)
    sin_pair = jnp.where(lane < CHARGES, swapped, coeff).astype(bf16)

    def at_x(s):
        return lax.rem(xi + NX - s, NX)

    for s in range(NX):
        mixture = sin_ref[s] * nn(cos_pair, qall[s]) - cos_ref[s] * nn(sin_pair, qall[s])
        for a in range(3):
            row = jnp.sum(twice(kb[4 + a]) * mixture, axis=0, keepdims=True)
            fsend[pl.ds(a * NX + at_x(s), 1), :] = row
    force_copies = {
        off: remote(fsend, frecv.at[off - 1], fsem.at[off - 1], frsem.at[off - 1], xpeer(off))
        for off in (2, 1, 3)
    }
    for copy in force_copies.values():
        copy.start()

    def paired(value):
        high, low = split(value)
        first = jnp.concatenate([high[0:CHARGES], low[0:CHARGES]], axis=0)
        second = jnp.concatenate([high[CHARGES:CHAN], low[CHARGES:CHAN]], axis=0)
        return first, second

    coeff_cos, coeff_sin = paired((kb[3] * coeff).T)

    for off in (1, 3, 2):
        force_copies[off].wait_recv()
    pulls = []
    for s in range(NX):
        rows = []
        for a in range(3):
            at = pl.ds(a * NX + at_x(s), 1)
            row = fsend[at, :] + frecv[0, at, :] + frecv[1, at, :] + frecv[2, at, :]
            row = row * steps[a]
            if s == 0:
                forces_ref[a : a + 1, :] = row
            rows.append(2.0 * (row - xpos[s, 3 + a : 4 + a, :]) * steps[a])
        pulls.append(rows)

    one = jnp.zeros((XROWS, CHAN), f32)
    two = jnp.zeros((XROWS, CHAN), f32)
    for s in range(NX):
        slopes = (
            twice(kb[0]) * pulls[s][0] + twice(kb[1]) * pulls[s][1] + twice(kb[2]) * pulls[s][2]
        )
        ssh_ref[s], ssl_ref[s] = split(slopes * sin_ref[s])
        sch_ref[s], scl_ref[s] = split(slopes * cos_ref[s])
        one = one + nn(ssh_ref[s], tq[s]) + nn(ssl_ref[s], tq[s])
        two = two + nn(sch_ref[s], tq[s]) + nn(scl_ref[s], tq[s])
    reduce_start(1, fold(one, -two))

    for s in range(NX):
        direct = (
            nn(coeff_cos, ssh_ref[s]) + nn(coeff_cos, ssl_ref[s])
            - nn(coeff_sin, sch_ref[s]) - nn(coeff_sin, scl_ref[s])
        )
        cg_ref[s] = direct[0:CHARGES] + direct[CHARGES:CHAN]
    reduce_finish(1)
    gather_finish(1)
    back_cos, back_sin = paired((kb[3] * res[1].astype(f32)).T)

    def charge_part(s):
        back = (
            nn(back_cos, ch_ref[s]) + nn(back_cos, cl_ref[s])
            + nn(back_sin, sh_ref[s]) + nn(back_sin, sl_ref[s])
        )
        return cg_ref[s] + (back[0:CHARGES] + back[CHARGES:CHAN])

    owner_copies = {}
    for s in (2, 1, 3):
        cgs[s - 1] = charge_part(s).astype(bf16)
        owner_copies[s] = remote(
            cgs.at[s - 1], cgr.at[s - 1], csend.at[s - 1], crecv.at[s - 1], xpeer(NX - s)
        )
        owner_copies[s].start()
    charge_grad = charge_part(0)
    for s in (1, 3, 2):
        owner_copies[s].wait_recv()
        charge_grad = charge_grad + cgr[s - 1].astype(f32)

    rounded = charge_grad.astype(bf16)
    pk[128:192, :] = nt(rounded, hidden_b)
    kinds = jnp.where(iota((8, ATOM), 0) == species, 1.0, 0.0).astype(bf16)
    gh, gl = split(charge_grad)
    pk[208:PACK, :] = jnp.zeros((PACK - 208, CHAN), f32)
    pk[208:216, 0:CHARGES] = nt(kinds, gh) + nt(kinds, gl)
    upstream = nn(cw, rounded)
    before_grad = (upstream * slope).astype(bf16)
    pk[0:128, :] = nt(messages_b, before_grad)
    message_grad = nn(mw_ref[...], before_grad).astype(bf16).astype(f32)
    lanes = iota((CHAN, CHAN), 1)
    radial_sum = jnp.zeros((CHAN, CHAN), f32)
    for b in range(BASIS):
        column = jnp.sum(message_grad * g_ref[b], axis=1, keepdims=True)
        radial_sum = jnp.where(lanes == b, column, radial_sum)
    pk[192:208, :] = radial_sum.T[0:BASIS, :]

    def p_rows(off):
        return pl.ds(pl.multiple_of(zat(off) * PROWS, PROWS), PROWS)

    def z3_copy(off):
        return remote(sg.at[p_rows(off)], rz3.at[off - 1], z3send.at[off - 1], z3recv.at[off - 1], zpeer(off))

    def x3_copy(off):
        return remote(xb3.at[xi], xb3.at[xi], x3send.at[off - 1], x3recv.at[off - 1], xpeer(off))

    def x3_arrival(off):
        theirs = lax.rem(xi + NX - off, NX)
        return remote(xb3.at[theirs], xb3.at[theirs], x3send.at[off - 1], x3recv.at[off - 1], xpeer(off))

    def a3_copy(off):
        mine = p_rows(0)
        return remote(res3.at[mine], res3.at[mine], a3send.at[off - 1], a3recv.at[off - 1], zpeer(off))

    def a3_arrival(off):
        theirs = p_rows(NZ - off)
        return remote(res3.at[theirs], res3.at[theirs], a3send.at[off - 1], a3recv.at[off - 1], zpeer(off))

    sg[...] = pk[...].astype(bf16)

    def z3_start(step, carry):
        z3_copy(far_first(step)).start()
        return carry

    def z3_take(step, total):
        off = far_first(NZ - 2 - step)
        z3_copy(off).wait_recv()
        return total + rz3[off - 1].astype(f32)

    lax.fori_loop(0, NZ - 1, z3_start, 0)
    xb3[xi] = lax.fori_loop(0, NZ - 1, z3_take, pk[p_rows(0), :])
    for off in (2, 1, 3):
        x3_copy(off).start()
    for off in (1, 3, 2):
        x3_arrival(off).wait_recv()
    res3[p_rows(0), :] = (xb3[0] + xb3[1] + xb3[2] + xb3[3]).astype(bf16)

    def a3_start(step, carry):
        a3_copy(far_first(step)).start()
        return carry

    def a3_take(step, carry):
        a3_arrival(far_first(NZ - 2 - step)).wait_recv()
        return carry

    lax.fori_loop(0, NZ - 1, a3_start, 0)
    lax.fori_loop(0, NZ - 1, a3_take, 0)

    total_ref[...] = res3[...]

    for copy in ghost_copies:
        copy.wait_send()
    for copies in (pos_copies, charge_copies, force_copies, owner_copies):
        for copy in copies.values():
            copy.wait_send()
    for off in range(1, NX):
        x3_copy(off).wait_send()

    def drain(off, carry):
        for t in range(2):
            z_copy(t, off).wait_send()
            a_copy(t, off).wait_send()
        z3_copy(off).wait_send()
        a3_copy(off).wait_send()
        return carry

    lax.fori_loop(1, NZ, drain, 0)


def finish(
    raw_ref, total_ref, forces_ref, rstep_ref, mstep_ref, cstep_ref, sstep_ref
):
    def scaled(rows, count):
        value = total_ref[rows, :].astype(f32)
        return value / jnp.sqrt(sum_all(value * value) * (1.0 / count) + 1e-06)

    forces_ref[...] = raw_ref[...]
    mstep_ref[...] = scaled(slice(0, 128), CHAN * CHAN)
    cstep_ref[...] = scaled(slice(128, 192), CHAN * CHARGES)
    rstep_ref[...] = scaled(slice(192, 208), BASIS * CHAN)
    sstep_ref[...] = scaled(slice(208, 224), SPECIES * CHARGES)[0:SPECIES, 0:CHARGES]


def on_device(
    features, positions, neighbours, neighbour_count, ghost_sends, species,
    wave_index, force_ref, radial_weight, mix_weight, charge_weight, species_charge,
):
    dma = pltpu.SemaphoreType.DMA
    vmem = pltpu.VMEM
    scratch = [
        vmem((ATOM, CHAN), bf16),
        vmem((3, ATOM), f32),
        vmem((SLOTS, ATOM), jnp.int32),
        vmem((1, ATOM), jnp.int32),
        vmem((2, ATOM), jnp.int32),
        vmem((1, ATOM), jnp.int32),
        vmem((3, WAVES), jnp.int32),
        vmem((3, ATOM), f32),
        vmem((BASIS, CHAN), bf16),
        vmem((CHAN, CHAN), bf16),
        vmem((CHARGES, CHAN), bf16),
        vmem((SPECIES, CHARGES), f32),
        dma((12,)),
        vmem((128, WAVES), f32),
        vmem((XROWS, 128), f32),
        vmem((7, XROWS, 128), f32),
        vmem((128, ATOM), f32),
        vmem((TABLE, 128), f32),
        vmem((128, 128), f32),
        *[vmem((NX, XROWS, ATOM), f32)] * 2,
        *[vmem((NX, XROWS, ATOM), bf16)] * 8,
        vmem((SLOTS, ATOM), jnp.int32),
        vmem((SLOTS, ATOM), jnp.int32),
        vmem((TABLE // 32, ATOM), jnp.int32),
        vmem((TABLE, ATOM), f32),
        vmem((TABLE, ATOM), f32),
        vmem((BASIS, ATOM, ATOM), bf16),
        vmem((BASIS, ATOM, ATOM), bf16),
        vmem((BASIS, CHAN, ATOM), f32),
        vmem((2, CHAN, ATOM), bf16),
        vmem((2, 8, ATOM), f32),
        vmem((2, CHAN, ATOM), bf16),
        vmem((2, 8, ATOM), f32),
        vmem((NX, 8, ATOM), f32),
        vmem((NX, CHAN, ATOM), bf16),
        vmem((NX, ATOM, CHAN), bf16),
        vmem((16, ATOM), f32),
        vmem((NX - 1, 16, ATOM), f32),
        vmem((NX, CHARGES, ATOM), f32),
        vmem((NX - 1, CHARGES, ATOM), bf16),
        vmem((NX - 1, CHARGES, ATOM), bf16),
        vmem((XROWS, CHAN), f32),
        vmem((2, XROWS, CHAN), bf16),
        vmem((2, NZ - 1, ZROWS, CHAN), bf16),
        vmem((2, XROWS, CHAN), bf16),
        vmem((PACK, CHAN), bf16),
        vmem((PACK, CHAN), f32),
        vmem((NZ - 1, PROWS, CHAN), bf16),
        vmem((NX, PROWS, CHAN), f32),
        vmem((PACK, CHAN), bf16),
        pltpu.SemaphoreType.REGULAR((3,)),
        dma((4,)),
        dma((4,)),
        *[dma((NX - 1,))] * 8,
        *[dma((2, NZ - 1))] * 4,
        dma((NZ - 1,)),
        dma((NZ - 1,)),
        dma((NX - 1,)),
        dma((NX - 1,)),
        dma((NZ - 1,)),
        dma((NZ - 1,)),
    ]
    spec = pl.BlockSpec(memory_space=pltpu.VMEM)
    raw, total = pl.pallas_call(
        kernel,
        out_shape=(
            jax.ShapeDtypeStruct((3, ATOM), f32),
            jax.ShapeDtypeStruct((PACK, CHAN), bf16),
        ),
        in_specs=[pl.BlockSpec(memory_space=pltpu.HBM)] * 12,
        out_specs=(spec,) * 2,
        scratch_shapes=scratch,
        compiler_params=pltpu.CompilerParams(
            collective_id=0, has_side_effects=True, vmem_limit_bytes=67043328
        ),
        name="step",
    )(
        features,
        positions,
        neighbours.T,
        neighbour_count.reshape(1, ATOM),
        ghost_sends,
        species.reshape(1, ATOM),
        wave_index,
        force_ref,
        radial_weight,
        mix_weight,
        charge_weight.T,
        species_charge,
    )
    forces, rstep, mstep, cstep, sstep = pl.pallas_call(
        finish,
        out_shape=(
            jax.ShapeDtypeStruct((3, ATOM), f32),
            jax.ShapeDtypeStruct((BASIS, CHAN), f32),
            jax.ShapeDtypeStruct((CHAN, CHAN), f32),
            jax.ShapeDtypeStruct((CHARGES, CHAN), f32),
            jax.ShapeDtypeStruct((SPECIES, CHARGES), f32),
        ),
        in_specs=[spec] * 2,
        out_specs=(spec,) * 5,
        compiler_params=pltpu.CompilerParams(vmem_limit_bytes=67043328),
        name="finish",
    )(raw, total)
    return forces, rstep, mstep, cstep.T, sstep


def solution(mesh):
    placed = (
        P(("cell", "dom"), None),
        P(None, ("cell", "dom")),
        P(("cell", "dom"), None),
        P(("cell", "dom")),
        P(None, ("cell", "dom")),
        P(("cell", "dom")),
        P(),
        P(None, ("cell", "dom")),
        P(),
        P(),
        P(),
        P(),
    )
    return jax.shard_map(
        on_device,
        mesh=mesh,
        in_specs=placed,
        out_specs=(
            P(None, ("cell", "dom")),
            P("cell", None),
            P("cell", None),
            P("cell", None),
            P("cell", None),
        ),
        check_vma=False,
    )
```

```python
import math

import jax
import jax.numpy as jnp
from jax import lax
from jax.experimental import pallas as pl
from jax.experimental.pallas import tpu as pltpu
from jax.sharding import PartitionSpec as P

f32 = jnp.float32
bf16 = jnp.bfloat16
MESH = pl.DeviceIdType.MESH

ATOM = 256
CHAN = 128
CHARGES = 64
WAVES = 1024
SLOTS = 64
BASIS = 16
SPECIES = 6
TABLE = 3 * ATOM
NX = 4
NZ = 16
DOMS = NX * NZ
TOTAL = ATOM * DOMS
XROWS = WAVES // NX
ZROWS = XROWS // NZ
PACK = 256
PROWS = PACK // NZ
SIDES = (1.25 * TOTAL / 64, 20.0, 20.0)
CUTOFF = 5.0
SPREAD = 2.0 * math.sqrt(math.log2(math.e))
GAP = 4.5 / 15
SHRINK = math.exp(-8.0 * GAP * GAP)
GROUP = 4
CENTERS = [0.5 + 4.5 * b / 15 for b in range(BASIS)]
COS_QUARTER = [(-1.0) ** n * (math.pi / 2) ** (2 * n) / math.factorial(2 * n) for n in range(8)]
SIN_HALF = [(-1.0) ** n * math.pi ** (2 * n + 1) / math.factorial(2 * n + 1) for n in range(8)]
COS_HALF = [(-1.0) ** n * math.pi ** (2 * n) / math.factorial(2 * n) for n in range(9)]


def nn(left, right):
    return lax.dot_general(left, right, (((1,), (0,)), ((), ())), preferred_element_type=f32)


def nt(left, right):
    return lax.dot_general(left, right, (((1,), (1,)), ((), ())), preferred_element_type=f32)


def split(value):
    high = value.astype(bf16)
    return high, (value - high.astype(f32)).astype(bf16)


def poly(coeffs, square):
    total = jnp.full_like(square, coeffs[-1])
    for coeff in reversed(coeffs[:-1]):
        total = total * square + coeff
    return total


def iota(shape, dim):
    return lax.broadcasted_iota(jnp.int32, shape, dim)


def sum_all(value):
    return jnp.sum(jnp.sum(value, axis=1, keepdims=True), axis=0, keepdims=True)


def kernel(
    feat_in, pos_in, nbr_in, cnt_in, ghost_in, spec_in, wave_in, fref_in,
    rw_in, mw_in, cwt_in, sc_in,
    forces_ref, total_ref,
    feat_ref, pos_ref, nbr_ref, cnt_ref, ghost_ref, spec_ref, wave_ref, fref_ref,
    rw_ref, mw_ref, cwt_ref, sc_ref, in_sem,
    wpad, wcol, kb, ppad, pcol, tpad, cos_ref, sin_ref, ch_ref, cl_ref, sh_ref, sl_ref,
    ssh_ref, ssl_ref, sch_ref, scl_ref, idx_ref, bit_ref, word_ref,
    mask_t, mask_ref, weight_ref, near_ref, ratio_ref, m_ref, ml_ref, g_ref, graw, gmeta,
    xpos, qall, tq, fsend, frecv, cg_ref, cgs, cgr,
    wave32, sz, rz, res, sg, pk, rz3, xb3, res3,
    rounds, gsend, grecv, psend, precv, qsend, qrecv, fsem, frsem, csend, crecv,
    zsend, zrecv, asend, arecv, z3send, z3recv, x3send, x3recv, a3send, a3recv,
):
    fetches = [
        pltpu.make_async_copy(src, dst, in_sem.at[i])
        for i, (src, dst) in enumerate((
            (feat_in, feat_ref), (pos_in, pos_ref), (ghost_in, ghost_ref), (fref_in, fref_ref),
            (wave_in, wave_ref), (nbr_in, nbr_ref), (cnt_in, cnt_ref), (rw_in, rw_ref),
            (mw_in, mw_ref), (cwt_in, cwt_ref), (sc_in, sc_ref), (spec_in, spec_ref),
        ))
    ]
    for copy in fetches:
        copy.start()
    me = lax.axis_index("dom")
    xi = lax.div(me, NZ)
    zi = lax.rem(me, NZ)
    upper = lax.rem(me + 1, DOMS)
    lower = lax.rem(me + DOMS - 1, DOMS)

    def xpeer(off):
        return lax.rem(xi + off, NX) * NZ + zi

    around = [zi] + [lax.rem(zi + off, NZ) for off in range(1, NZ)]

    def zat(off):
        return around[off % NZ]

    def far_first(step):
        return NZ // 2 + (1 - 2 * (step % 2)) * ((step + 1) // 2)

    def each(body, carry):
        for step in range(NZ - 1):
            carry = body(step, carry)
        return carry

    def zpeer(off):
        return xi * NZ + zat(off)

    barrier = pltpu.get_barrier_semaphore()

    def greet(target):
        pl.semaphore_signal(barrier, inc=1, device_id={"dom": target}, device_id_type=MESH)

    for off in range(1, NX):
        greet(xpeer(off))
    greet(upper)
    greet(lower)
    greet(zpeer(1))
    greet(zpeer(NZ - 1))

    def reach_tell(level):
        for off in (2**level, NZ - 2**level):
            pl.semaphore_signal(
                rounds.at[level], inc=1, device_id={"dom": zpeer(off)}, device_id_type=MESH
            )

    def reach_learn(level):
        pl.semaphore_wait(rounds.at[level], 2)

    def remote(src, dst, send, recv, target):
        return pltpu.make_async_remote_copy(
            src_ref=src, dst_ref=dst, send_sem=send, recv_sem=recv,
            device_id={"dom": target}, device_id_type=MESH,
        )

    for copy in fetches[:5]:
        copy.wait()

    xpos[0, 0:3, :] = pos_ref[...]
    xpos[0, 3:6, :] = fref_ref[...]
    xpos[0, 6:8, :] = ghost_ref[...].astype(f32)

    pl.semaphore_wait(barrier, NX - 1 + 4)

    ghost_copies = []
    for slot, target in ((0, upper), (1, lower)):
        ghost_copies.append(
            remote(xpos.at[0], gmeta.at[slot], gsend.at[2 * slot], grecv.at[2 * slot], target)
        )
        ghost_copies.append(
            remote(feat_ref, graw.at[slot], gsend.at[2 * slot + 1], grecv.at[2 * slot + 1], target)
        )

    def x_message(src, dst_ref, send, recv, off):
        return remote(src, dst_ref.at[off], send.at[off - 1], recv.at[off - 1], xpeer(off))

    for copy in ghost_copies:
        copy.start()
    reach_tell(0)
    pos_copies = {off: x_message(xpos.at[0], xpos, psend, precv, off) for off in (2, 1, 3)}
    for copy in pos_copies.values():
        copy.start()

    for copy in fetches[5:]:
        copy.wait()
    ft32 = feat_ref[...].astype(f32).T
    tpad[...] = jnp.zeros_like(tpad)
    ppad[...] = jnp.zeros_like(ppad)
    ppad[0:3, :] = pos_ref[...]
    pcol[...] = ppad[...].T

    wave = wave_ref[...].astype(f32)
    wpad[...] = jnp.zeros_like(wpad)
    wpad[0:3, :] = wave
    steps = [2.0 * math.pi / side for side in SIDES]
    square = sum((wave[a : a + 1, :] * steps[a]) ** 2 for a in range(3))
    wpad[3:4, :] = jnp.exp(-0.5 * square) * (1.0 / TOTAL)
    mine = pl.ds(pl.multiple_of(xi * XROWS, XROWS), XROWS)
    wcol[...] = wpad[:, mine].T
    damp_col = jnp.broadcast_to(wcol[:, 3:4], (XROWS, 128))
    kb[3] = damp_col
    for a in range(3):
        spread = jnp.broadcast_to(wcol[:, a : a + 1], (XROWS, 128))
        kb[a] = spread
        kb[4 + a] = spread * damp_col

    def twice(value):
        return jnp.concatenate([value, value], axis=1)

    def phases(block):
        own = xpos[block]
        tx, ty, tz = (own[a : a + 1, :] * (1.0 / SIDES[a]) for a in range(3))

        def phase_block(step, carry):
            rows = pl.ds(pl.multiple_of(step * 32, 32), 32)
            turns = (
                twice(kb[0, rows, :]) * tx + twice(kb[1, rows, :]) * ty + twice(kb[2, rows, :]) * tz
            )
            turns = turns - jnp.floor(turns + 0.5)
            sq = turns * turns
            half_sin = turns * poly(SIN_HALF, sq)
            half_cos = poly(COS_HALF, sq)
            cosine = 1.0 - 2.0 * half_sin * half_sin
            sine = 2.0 * half_sin * half_cos
            cos_ref[block, rows, :] = cosine
            sin_ref[block, rows, :] = sine
            ch_ref[block, rows, :], cl_ref[block, rows, :] = split(cosine)
            sh_ref[block, rows, :], sl_ref[block, rows, :] = split(sine)
            return carry

        lax.fori_loop(0, XROWS // 32, phase_block, 0)

    phases(0)

    entries = nbr_ref[...]
    live = iota((SLOTS, ATOM), 0) < cnt_ref[...]
    idx_ref[...] = jnp.where(live, lax.shift_right_logical(entries, 5), -1)
    bit_ref[...] = lax.shift_left(jnp.ones_like(entries), entries & 31)
    word_rows = iota((TABLE // 32, ATOM), 0)

    def word_step(n, words):
        hit = word_rows == idx_ref[pl.ds(n, 1), :]
        return words | jnp.where(hit, bit_ref[pl.ds(n, 1), :], 0)

    word_ref[...] = lax.fori_loop(
        0, SLOTS, word_step, jnp.zeros((TABLE // 32, ATOM), jnp.int32)
    )

    reach_learn(0)
    reach_tell(1)

    def mask_step(step, carry):
        bits = lax.shift_right_logical(
            jnp.broadcast_to(word_ref[pl.ds(step, 1), :], (32, ATOM)), iota((32, ATOM), 0)
        ) & 1
        rows = pl.ds(pl.multiple_of(step * 32, 32), 32)
        mask_t[rows, :] = bits.astype(f32)
        return carry

    lax.fori_loop(0, TABLE // 32, mask_step, 0)
    for block in range(3):
        mask_ref[block] = mask_t[block * ATOM : (block + 1) * ATOM, :].T

    def edge_sums(block, others, feats):
        def edge_block(step, carry):
            rows = pl.ds(pl.multiple_of(step * 32, 32), 32)
            cols = pcol[rows, :]
            dist2 = jnp.zeros((32, ATOM), f32)
            for a in range(3):
                delta = others[a : a + 1, :] - cols[:, a : a + 1]
                delta = delta - SIDES[a] * jnp.floor(delta * (1.0 / SIDES[a]) + 0.5)
                dist2 = dist2 + delta * delta
            dist = jnp.sqrt(dist2)
            near = jnp.minimum(dist, CUTOFF)
            part = near * (1.0 / CUTOFF)
            fade = poly(COS_QUARTER, part * part)
            fade = jnp.where(dist < CUTOFF, fade * fade, 0.0)
            weight_ref[block, rows, :] = fade * mask_ref[block, rows, :]
            near_ref[block, rows, :] = near * SPREAD
            ratio_ref[block, rows, :] = jnp.exp((8.0 * GAP) * (near - CENTERS[0]) - 4.0 * GAP * GAP)
            return carry

        lax.fori_loop(0, ATOM // 32, edge_block, 0)
        for first in range(0, BASIS, GROUP):
            for start in range(0, ATOM, 32):
                at = slice(start, start + 32)
                away = near_ref[block, at, :] - SPREAD * CENTERS[first]
                weight = weight_ref[block, at, :]
                ratio = ratio_ref[block, at, :] * SHRINK**first
                basis = jnp.exp2(-(away * away))
                for b in range(first, first + GROUP):
                    high, low = split(basis.astype(bf16).astype(f32) * weight)
                    m_ref[b, at, :] = high
                    ml_ref[b, at, :] = low
                    if b + 1 < first + GROUP:
                        basis = basis * ratio
                        ratio = ratio * SHRINK
            for b in range(first, first + GROUP):
                fresh = nn(m_ref[b], feats) + nn(ml_ref[b], feats)
                g_ref[b] = fresh if block == 0 else g_ref[b] + fresh

    edge_sums(0, pos_ref[...], feat_ref[...])
    reach_learn(1)
    reach_tell(2)

    for copy in ghost_copies:
        copy.wait_recv()
    rows_of = iota((ATOM, ATOM), 0).astype(f32)
    for slot in range(2):
        meta = gmeta[slot]
        perm32 = jnp.where(rows_of == meta[7 - slot : 8 - slot, :], 1.0, 0.0)
        perm = perm32.astype(bf16)
        p1 = meta.astype(bf16)
        p2 = (meta - p1.astype(f32)).astype(bf16)
        p3 = (meta - p1.astype(f32) - p2.astype(f32)).astype(bf16)
        coords = nn(p1, perm) + nn(p2, perm) + nn(p3, perm)
        edge_sums(1 + slot, coords, nn(perm32.T.astype(bf16), graw[slot]).astype(bf16))

    radial = rw_ref[...].astype(f32)
    messages = jnp.zeros((ATOM, CHAN), f32)
    for b in range(BASIS):
        messages = messages + radial[b : b + 1, :] * g_ref[b]
    messages_b = messages.T.astype(bf16)
    mixT = mw_ref[...].astype(f32).T.astype(bf16)
    before = nn(mixT, messages_b)
    sigmoid = 1.0 / (1.0 + jnp.exp(-before))
    hidden_b = (ft32 + before * sigmoid).astype(bf16)
    slope = sigmoid * (1.0 + before * (1.0 - sigmoid))
    cwT = cwt_ref[...]
    tpad[0:CHARGES, :] = cwT.astype(f32)
    cw = tpad[...].T[:, 0:CHARGES].astype(bf16)
    tpad[...] = jnp.zeros_like(tpad)
    tpad[0:SPECIES, 0:CHARGES] = sc_ref[...]
    offsets = tpad[...].T[0:CHARGES, :]
    species = spec_ref[...]
    charges = nn(cwT, hidden_b)
    added = jnp.zeros((CHARGES, ATOM), f32)
    for s in range(SPECIES):
        added = jnp.where(species == s, offsets[:, s : s + 1], added)
    qall[0, 0:CHARGES, :], qall[0, CHARGES:CHAN, :] = split(charges + added)
    charge_copies = {off: x_message(qall.at[0], qall, qsend, qrecv, off) for off in (2, 1, 3)}
    for copy in charge_copies.values():
        copy.start()

    for off in (1, 3, 2):
        pos_copies[off].wait_recv()
        phases(off)

    lane = iota((XROWS, CHAN), 1)

    def fold(one, two):
        one = one + pltpu.roll(one, CHARGES, 1)
        two = two + pltpu.roll(two, CHARGES, 1)
        return jnp.where(lane < CHARGES, one, two)

    def z_rows(off):
        return pl.ds(pl.multiple_of(zat(off) * ZROWS, ZROWS), ZROWS)

    def z_copy(t, off):
        return remote(
            sz.at[t, z_rows(off)], rz.at[t, off - 1], zsend.at[t, off - 1], zrecv.at[t, off - 1], zpeer(off)
        )

    def a_copy(t, off):
        rows = z_rows(0)
        return remote(
            res.at[t, rows], res.at[t, rows], asend.at[t, off - 1], arecv.at[t, off - 1], zpeer(off)
        )

    def a_arrival(t, off):
        rows = z_rows(NZ - off)
        return remote(
            res.at[t, rows], res.at[t, rows], asend.at[t, off - 1], arecv.at[t, off - 1], zpeer(off)
        )

    def reduce_start(t, partial):
        wave32[...] = partial
        sz[t] = partial.astype(bf16)

        def z_start(step, carry):
            z_copy(t, far_first(step)).start()
            return carry

        each(z_start, 0)

    def reduce_finish(t):
        def z_take(step, total):
            off = far_first(NZ - 2 - step)
            z_copy(t, off).wait_recv()
            return total + rz[t, off - 1].astype(f32)

        total = each(z_take, wave32[z_rows(0), :])
        res[t, z_rows(0), :] = total.astype(bf16)

        def a_start(step, carry):
            a_copy(t, far_first(step)).start()
            return carry

        each(a_start, 0)

    def gather_finish(t):
        def a_take(step, carry):
            a_arrival(t, far_first(NZ - 2 - step)).wait_recv()
            return carry

        each(a_take, 0)

    one = jnp.zeros((XROWS, CHAN), f32)
    two = jnp.zeros((XROWS, CHAN), f32)
    for s in (0, 1, 3, 2):
        if s:
            charge_copies[s].wait_recv()
        tq[s] = qall[s].astype(f32).T.astype(bf16)
        one = one + nn(ch_ref[s], tq[s]) + nn(cl_ref[s], tq[s])
        two = two + nn(sh_ref[s], tq[s]) + nn(sl_ref[s], tq[s])
    reach_learn(2)
    reduce_start(0, fold(one, two))
    reduce_finish(0)
    gather_finish(0)

    coeff = res[0].astype(f32)
    swapped = pltpu.roll(coeff, CHARGES, 1)
    cos_pair = jnp.where(lane < CHARGES, coeff, swapped).astype(bf16)
    sin_pair = jnp.where(lane < CHARGES, swapped, coeff).astype(bf16)

    def at_x(s):
        return lax.rem(xi + NX - s, NX)

    for s in range(NX):
        mixture = sin_ref[s] * nn(cos_pair, qall[s]) - cos_ref[s] * nn(sin_pair, qall[s])
        for a in range(3):
            row = jnp.sum(twice(kb[4 + a]) * mixture, axis=0, keepdims=True)
            fsend[pl.ds(a * NX + at_x(s), 1), :] = row
    force_copies = {
        off: remote(fsend, frecv.at[off - 1], fsem.at[off - 1], frsem.at[off - 1], xpeer(off))
        for off in (2, 1, 3)
    }
    for copy in force_copies.values():
        copy.start()

    def paired(value):
        high, low = split(value)
        first = jnp.concatenate([high[0:CHARGES], low[0:CHARGES]], axis=0)
        second = jnp.concatenate([high[CHARGES:CHAN], low[CHARGES:CHAN]], axis=0)
        return first, second

    coeff_cos, coeff_sin = paired((kb[3] * coeff).T)

    for off in (1, 3, 2):
        force_copies[off].wait_recv()
    pulls = []
    for s in range(NX):
        rows = []
        for a in range(3):
            at = pl.ds(a * NX + at_x(s), 1)
            row = fsend[at, :] + frecv[0, at, :] + frecv[1, at, :] + frecv[2, at, :]
            row = row * steps[a]
            if s == 0:
                forces_ref[a : a + 1, :] = row
            rows.append(2.0 * (row - xpos[s, 3 + a : 4 + a, :]) * steps[a])
        pulls.append(rows)

    one = jnp.zeros((XROWS, CHAN), f32)
    two = jnp.zeros((XROWS, CHAN), f32)
    for s in range(NX):
        slopes = (
            twice(kb[0]) * pulls[s][0] + twice(kb[1]) * pulls[s][1] + twice(kb[2]) * pulls[s][2]
        )
        ssh_ref[s], ssl_ref[s] = split(slopes * sin_ref[s])
        sch_ref[s], scl_ref[s] = split(slopes * cos_ref[s])
        one = one + nn(ssh_ref[s], tq[s]) + nn(ssl_ref[s], tq[s])
        two = two + nn(sch_ref[s], tq[s]) + nn(scl_ref[s], tq[s])
    reduce_start(1, fold(one, -two))

    for s in range(NX):
        direct = (
            nn(coeff_cos, ssh_ref[s]) + nn(coeff_cos, ssl_ref[s])
            - nn(coeff_sin, sch_ref[s]) - nn(coeff_sin, scl_ref[s])
        )
        cg_ref[s] = direct[0:CHARGES] + direct[CHARGES:CHAN]
    reduce_finish(1)
    gather_finish(1)
    back_cos, back_sin = paired((kb[3] * res[1].astype(f32)).T)

    def charge_part(s):
        back = (
            nn(back_cos, ch_ref[s]) + nn(back_cos, cl_ref[s])
            + nn(back_sin, sh_ref[s]) + nn(back_sin, sl_ref[s])
        )
        return cg_ref[s] + (back[0:CHARGES] + back[CHARGES:CHAN])

    owner_copies = {}
    for s in (2, 1, 3):
        cgs[s - 1] = charge_part(s).astype(bf16)
        owner_copies[s] = remote(
            cgs.at[s - 1], cgr.at[s - 1], csend.at[s - 1], crecv.at[s - 1], xpeer(NX - s)
        )
        owner_copies[s].start()
    charge_grad = charge_part(0)
    for s in (1, 3, 2):
        owner_copies[s].wait_recv()
        charge_grad = charge_grad + cgr[s - 1].astype(f32)

    rounded = charge_grad.astype(bf16)
    pk[128:192, :] = nt(rounded, hidden_b)
    kinds = jnp.where(iota((8, ATOM), 0) == species, 1.0, 0.0).astype(bf16)
    gh, gl = split(charge_grad)
    pk[208:PACK, :] = jnp.zeros((PACK - 208, CHAN), f32)
    pk[208:216, 0:CHARGES] = nt(kinds, gh) + nt(kinds, gl)
    upstream = nn(cw, rounded)
    before_grad = (upstream * slope).astype(bf16)
    pk[0:128, :] = nt(messages_b, before_grad)
    message_grad = nn(mw_ref[...], before_grad).astype(bf16).astype(f32).T
    for b in range(BASIS):
        pk[192 + b : 193 + b, :] = jnp.sum(message_grad * g_ref[b], axis=0, keepdims=True)

    def p_rows(off):
        return pl.ds(pl.multiple_of(zat(off) * PROWS, PROWS), PROWS)

    def z3_copy(off):
        return remote(sg.at[p_rows(off)], rz3.at[off - 1], z3send.at[off - 1], z3recv.at[off - 1], zpeer(off))

    def x3_copy(off):
        return remote(xb3.at[xi], xb3.at[xi], x3send.at[off - 1], x3recv.at[off - 1], xpeer(off))

    def x3_arrival(off):
        theirs = lax.rem(xi + NX - off, NX)
        return remote(xb3.at[theirs], xb3.at[theirs], x3send.at[off - 1], x3recv.at[off - 1], xpeer(off))

    def a3_copy(off):
        mine = p_rows(0)
        return remote(res3.at[mine], res3.at[mine], a3send.at[off - 1], a3recv.at[off - 1], zpeer(off))

    def a3_arrival(off):
        theirs = p_rows(NZ - off)
        return remote(res3.at[theirs], res3.at[theirs], a3send.at[off - 1], a3recv.at[off - 1], zpeer(off))

    sg[...] = pk[...].astype(bf16)

    def z3_start(step, carry):
        z3_copy(far_first(step)).start()
        return carry

    def z3_take(step, total):
        off = far_first(NZ - 2 - step)
        z3_copy(off).wait_recv()
        return total + rz3[off - 1].astype(f32)

    each(z3_start, 0)
    xb3[xi] = each(z3_take, pk[p_rows(0), :])
    for off in (2, 1, 3):
        x3_copy(off).start()
    for off in (1, 3, 2):
        x3_arrival(off).wait_recv()
    res3[p_rows(0), :] = (xb3[0] + xb3[1] + xb3[2] + xb3[3]).astype(bf16)

    def a3_start(step, carry):
        a3_copy(far_first(step)).start()
        return carry

    def a3_take(step, carry):
        a3_arrival(far_first(NZ - 2 - step)).wait_recv()
        return carry

    each(a3_start, 0)
    each(a3_take, 0)

    total_ref[...] = res3[...]

    for copy in ghost_copies:
        copy.wait_send()
    for copies in (pos_copies, charge_copies, force_copies, owner_copies):
        for copy in copies.values():
            copy.wait_send()
    for off in range(1, NX):
        x3_copy(off).wait_send()

    def drain(off, carry):
        for t in range(2):
            z_copy(t, off).wait_send()
            a_copy(t, off).wait_send()
        z3_copy(off).wait_send()
        a3_copy(off).wait_send()
        return carry

    for off in range(1, NZ):
        drain(off, 0)


def finish(
    raw_ref, total_ref, forces_ref, rstep_ref, mstep_ref, cstep_ref, sstep_ref
):
    def scaled(rows, count):
        value = total_ref[rows, :].astype(f32)
        return value / jnp.sqrt(sum_all(value * value) * (1.0 / count) + 1e-06)

    forces_ref[...] = raw_ref[...]
    mstep_ref[...] = scaled(slice(0, 128), CHAN * CHAN)
    cstep_ref[...] = scaled(slice(128, 192), CHAN * CHARGES)
    rstep_ref[...] = scaled(slice(192, 208), BASIS * CHAN)
    sstep_ref[...] = scaled(slice(208, 224), SPECIES * CHARGES)[0:SPECIES, 0:CHARGES]


def on_device(
    features, positions, neighbours, neighbour_count, ghost_sends, species,
    wave_index, force_ref, radial_weight, mix_weight, charge_weight, species_charge,
):
    dma = pltpu.SemaphoreType.DMA
    vmem = pltpu.VMEM
    scratch = [
        vmem((ATOM, CHAN), bf16),
        vmem((3, ATOM), f32),
        vmem((SLOTS, ATOM), jnp.int32),
        vmem((1, ATOM), jnp.int32),
        vmem((2, ATOM), jnp.int32),
        vmem((1, ATOM), jnp.int32),
        vmem((3, WAVES), jnp.int32),
        vmem((3, ATOM), f32),
        vmem((BASIS, CHAN), bf16),
        vmem((CHAN, CHAN), bf16),
        vmem((CHARGES, CHAN), bf16),
        vmem((SPECIES, CHARGES), f32),
        dma((12,)),
        vmem((128, WAVES), f32),
        vmem((XROWS, 128), f32),
        vmem((7, XROWS, 128), f32),
        vmem((128, ATOM), f32),
        vmem((ATOM, 128), f32),
        vmem((128, 128), f32),
        *[vmem((NX, XROWS, ATOM), f32)] * 2,
        *[vmem((NX, XROWS, ATOM), bf16)] * 8,
        vmem((SLOTS, ATOM), jnp.int32),
        vmem((SLOTS, ATOM), jnp.int32),
        vmem((TABLE // 32, ATOM), jnp.int32),
        vmem((TABLE, ATOM), f32),
        *[vmem((3, ATOM, ATOM), f32)] * 4,
        vmem((BASIS, ATOM, ATOM), bf16),
        vmem((BASIS, ATOM, ATOM), bf16),
        vmem((BASIS, ATOM, CHAN), f32),
        vmem((2, ATOM, CHAN), bf16),
        vmem((2, 8, ATOM), f32),
        vmem((NX, 8, ATOM), f32),
        vmem((NX, CHAN, ATOM), bf16),
        vmem((NX, ATOM, CHAN), bf16),
        vmem((16, ATOM), f32),
        vmem((NX - 1, 16, ATOM), f32),
        vmem((NX, CHARGES, ATOM), f32),
        vmem((NX - 1, CHARGES, ATOM), bf16),
        vmem((NX - 1, CHARGES, ATOM), bf16),
        vmem((XROWS, CHAN), f32),
        vmem((2, XROWS, CHAN), bf16),
        vmem((2, NZ - 1, ZROWS, CHAN), bf16),
        vmem((2, XROWS, CHAN), bf16),
        vmem((PACK, CHAN), bf16),
        vmem((PACK, CHAN), f32),
        vmem((NZ - 1, PROWS, CHAN), bf16),
        vmem((NX, PROWS, CHAN), f32),
        vmem((PACK, CHAN), bf16),
        pltpu.SemaphoreType.REGULAR((3,)),
        dma((4,)),
        dma((4,)),
        *[dma((NX - 1,))] * 8,
        *[dma((2, NZ - 1))] * 4,
        dma((NZ - 1,)),
        dma((NZ - 1,)),
        dma((NX - 1,)),
        dma((NX - 1,)),
        dma((NZ - 1,)),
        dma((NZ - 1,)),
    ]
    spec = pl.BlockSpec(memory_space=pltpu.VMEM)
    raw, total = pl.pallas_call(
        kernel,
        out_shape=(
            jax.ShapeDtypeStruct((3, ATOM), f32),
            jax.ShapeDtypeStruct((PACK, CHAN), bf16),
        ),
        in_specs=[pl.BlockSpec(memory_space=pltpu.HBM)] * 12,
        out_specs=(spec,) * 2,
        scratch_shapes=scratch,
        compiler_params=pltpu.CompilerParams(
            collective_id=0, has_side_effects=True, vmem_limit_bytes=67043328
        ),
        name="step",
    )(
        features,
        positions,
        neighbours.T,
        neighbour_count.reshape(1, ATOM),
        ghost_sends,
        species.reshape(1, ATOM),
        wave_index,
        force_ref,
        radial_weight,
        mix_weight,
        charge_weight.T,
        species_charge,
    )
    forces, rstep, mstep, cstep, sstep = pl.pallas_call(
        finish,
        out_shape=(
            jax.ShapeDtypeStruct((3, ATOM), f32),
            jax.ShapeDtypeStruct((BASIS, CHAN), f32),
            jax.ShapeDtypeStruct((CHAN, CHAN), f32),
            jax.ShapeDtypeStruct((CHARGES, CHAN), f32),
            jax.ShapeDtypeStruct((SPECIES, CHARGES), f32),
        ),
        in_specs=[spec] * 2,
        out_specs=(spec,) * 5,
        compiler_params=pltpu.CompilerParams(vmem_limit_bytes=67043328),
        name="finish",
    )(raw, total)
    return forces, rstep, mstep, cstep.T, sstep


def solution(mesh):
    placed = (
        P(("cell", "dom"), None),
        P(None, ("cell", "dom")),
        P(("cell", "dom"), None),
        P(("cell", "dom")),
        P(None, ("cell", "dom")),
        P(("cell", "dom")),
        P(),
        P(None, ("cell", "dom")),
        P(),
        P(),
        P(),
        P(),
    )
    return jax.shard_map(
        on_device,
        mesh=mesh,
        in_specs=placed,
        out_specs=(
            P(None, ("cell", "dom")),
            P("cell", None),
            P("cell", None),
            P("cell", None),
            P("cell", None),
        ),
        check_vma=False,
    )
```
